32 devices in a mesh: pb: 8 (over y, x, core), pa: 4 (over z).
Axes of the slice: x: 2, y: 2, z: 4, core: 2. Of those that a mesh axis runs over, the one named last changes fastest.
Arguments:
- query_states: bfloat16 [2048, 768], P(('pb', 'pa')), may hold values from -6 to 6
- passage_states: bfloat16 [24576, 768], P(('pb', 'pa')), may hold values from -6 to 6
- passage_bins: int32 [32, 768], P(('pb', 'pa')), may hold values from 0 to 3, never falling along the last dimension, each value on 1 to 512 neighbouring positions
- padding_mask: int32 [32, 768], P(('pb', 'pa')), may hold values 0 or 1
- token_ids: int32 [32, 768], P(('pb', 'pa')), may hold values from 0 to 30521
- positives: int32 [64], replicated, may hold values from 0 to 127
- united_weight: bfloat16 [768, 2304], replicated, may hold values from -0.21875 to 0.21875
- output_weight: bfloat16 [768, 768], replicated, may hold values from -0.875 to 0.875
- first_gain: float32 [768], replicated, may hold values from 0.1 to 1.9
- first_shift: float32 [768], replicated, may hold values from -3 to 3
- up_weight: bfloat16 [768, 3072], replicated, may hold values from -0.21875 to 0.21875
- up_bias: float32 [3072], replicated, may hold values from -3 to 3
- down_weight: bfloat16 [3072, 768], replicated, may hold values from -0.109375 to 0.109375
- second_gain: float32 [768], replicated, may hold values from 0.1 to 1.9
- second_shift: float32 [768], replicated, may hold values from -3 to 3
- project_weight: bfloat16 [768, 128], replicated, may hold values from -0.21875 to 0.21875
Outputs:
- query_embeddings: bfloat16 [2048, 128], P(('pb', 'pa'))
- passage_embeddings: bfloat16 [24576, 128], P(('pb', 'pa'))
- query_losses: float32 [64], P(('pb', 'pa'))
- grad_query_states: float32 [2048, 768], P(('pb', 'pa'))
- grad_passage_states: float32 [24576, 768], P(('pb', 'pa'))
- grad_united: float32 [768, 2304], P(('pb', 'pa'))
- grad_output: float32 [768, 768], P(('pb', 'pa'))
- grad_first_gain: float32 [768], P(('pb', 'pa'))
- grad_first_shift: float32 [768], P(('pb', 'pa'))
- grad_up: float32 [768, 3072], P(('pb', 'pa'))
- grad_up_bias: float32 [3072], P(('pb', 'pa'))
- grad_down: float32 [3072, 768], P(('pb', 'pa'))
- grad_second_gain: float32 [768], P(('pb', 'pa'))
- grad_second_shift: float32 [768], P(('pb', 'pa'))
- grad_project: float32 [768, 128], P(('pb', 'pa'))
The draws below stay inside these ranges and needn't reach their ends.
Inputs may be any that keep to these rules, and one draw needn't show every extreme that they name: `passage_bins`: within each row of 768 tokens the bin numbers never fall, every bin holds 1 to 512 tokens, and one bin holds exactly 512.
All inputs are finite; a program needn't handle non-finite values. No bound on the sum of `padding_mask` on one device may be relied on, other than what follows from the above.
Results may differ from the reference program's by a relative error of at most 0.014.
Values may be sent and summed in bfloat16 or wider, within the bound.
No kernel may reach another device: no remote copies, remote signals or barrier semaphores. Data moves between devices by JAX's collectives and lax.ppermute only.
A program may use at most 320 MiB of HBM per device.

```python
import math
import jax
import jax.numpy as jnp
import numpy as np
from jax import lax

D = 768
HEAD_DIM = 64
HEADS = 12
FF = 3072
PROJ = 128
QLEN = 32
VOCAB = 30522
PTOK_DEV = 768
PSG_DEV = 4
PLEN_MAX = 512
SKIP_IDS = 3000
NQ = 64
NQTOK = 2048
NPSG = 128
NPTOK = 24576
N_PB = 8
N_PA = 4


def set_ends(array, stream_key, least, largest):
    extent = array.shape
    spot = [jax.random.randint(jax.random.fold_in(stream_key, axis), (), 0, extent[axis]) for axis in range(len(extent))]
    array = array.at[tuple(spot)].set(least)
    longest = extent.index(max(extent))
    spot[longest] = (spot[longest] + 1) % extent[longest]
    return array.at[tuple(spot)].set(largest)


def shard_levels(rng, shape, shards, least, largest):
    def one(dim, parts):
        heights = jax.random.uniform(jax.random.fold_in(jax.random.fold_in(rng, 6), dim), (parts,), jnp.float32, least / len(shards), largest / len(shards))
        return jnp.repeat(jnp.exp(heights), shape[dim] // parts).reshape((-1,) + (1,) * (len(shape) - dim - 1))

    loudness = one(*shards[0])
    for cut in shards[1:]:
        loudness = loudness * one(*cut)
    return loudness


def cumulative_ranks(count, skew):
    loads = [(1 << 20) // math.isqrt(standing ** skew) + 1 for standing in range(1, count + 1)]
    deviation = 1 + sum(loads) // (1 << 30)
    return np.cumsum(np.array([max(1, weight // deviation) for weight in loads]))


def ranked_ids(own_key, extent, amount, skew):
    grid = cumulative_ranks(amount, skew)
    pick = jax.random.randint(jax.random.fold_in(own_key, 1), extent, 0, int(grid[amount - 1]))
    rank = jnp.searchsorted(jnp.asarray(grid, jnp.int32), pick, side="right")
    return jax.random.permutation(jax.random.fold_in(own_key, 2), amount)[rank].astype(jnp.int32)


def split_up(amount, total, limit, skew):
    loads = [(1 << 20) // math.isqrt(rank ** skew) + 1 for rank in range(2, amount + 1)]
    rest, counts = total - limit - (amount - 1), [1] * (amount - 1)
    while rest > 0:
        free = [i for i in range(amount - 1) if counts[i] < limit]
        pool, budget = sum([loads[i] for i in free]), rest
        for i in free:
            addition = min(limit - counts[i], max(1, budget * loads[i] // pool), rest)
            counts[i] = counts[i] + addition
            rest = rest - addition
    return np.array([limit] + counts)


def ragged(stream_key, count, total, limit, skew):
    if count == 2:
        one = jax.random.randint(stream_key, (), max(1, total - limit), min(limit, total - 1) + 1)
        return jnp.stack([one, total - one])
    lengths = jnp.asarray(split_up(count, total, limit, skew), jnp.int32)
    couples = (count - 1) // 2
    donor, sink = lengths[1:1 + 2 * couples:2], lengths[2:2 + 2 * couples:2]
    room = jnp.minimum(donor - 1, limit - sink)
    passed = jax.random.randint(jax.random.fold_in(stream_key, 1), (couples,), 0, 1 << 20) % (room + 1)
    lengths = lengths.at[1:1 + 2 * couples:2].set(donor - passed).at[2:2 + 2 * couples:2].set(sink + passed)
    return lengths[jax.random.permutation(jax.random.fold_in(stream_key, 2), count)]


def bell_draw(own_key, shape, width, most, shards=(), held_as=jnp.bfloat16):
    gain = shard_levels(own_key, shape, shards, -0.22, 0.18) if shards else 1.0
    values = jax.random.normal(own_key, shape, jnp.float32) * width * gain
    return jnp.minimum(jnp.maximum(values, -most), most).astype(held_as)


def setup_inputs(seed: int = 0) -> dict:
    key_list = jax.random.split(jax.random.key(seed), 17)
    query_states = bell_draw(key_list[0], (NQTOK, D), 1.0, 6.0, ((0, 32),))
    passage_states = bell_draw(key_list[1], (NPTOK, D), 1.0, 6.0, ((0, 32),))
    passage_bins = jax.vmap(lambda own: jnp.searchsorted(jnp.cumsum(ragged(own, PSG_DEV, PTOK_DEV, PLEN_MAX, 2)), jnp.arange(PTOK_DEV), side="right"))(jax.random.split(key_list[2], (N_PB * N_PA))).reshape((N_PB * N_PA, PTOK_DEV)).astype(jnp.int32)
    padding_mask = set_ends((jax.random.randint(key_list[3], (N_PB * N_PA, PTOK_DEV), 0, 8) < 7).astype(jnp.int32), jax.random.fold_in(key_list[3], 1), 0, 1)
    token_ids = set_ends(ranked_ids(key_list[4], (N_PB * N_PA, PTOK_DEV), VOCAB, 2), jax.random.fold_in(key_list[4], 3), 0, VOCAB - 1).astype(jnp.int32)
    positives = set_ends(jax.random.randint(key_list[5], (NQ,), 0, NPSG), jax.random.fold_in(key_list[5], 1), 0, NPSG - 1).astype(jnp.int32)
    united_weight = bell_draw(key_list[6], (D, 3 * D), D ** -0.5, 0.21875)
    output_weight = bell_draw(key_list[7], (D, D), (D // 16) ** -0.5, 0.875)
    first_gain = jnp.clip(1.0 + 0.18 * jax.random.normal(key_list[8], (D,), jnp.float32), 0.1, 1.9)
    first_shift = bell_draw(key_list[9], (D,), 0.5, 3.0, (), jnp.float32)
    up_weight = bell_draw(key_list[10], (D, FF), D ** -0.5, 0.21875)
    up_bias = bell_draw(key_list[11], (FF,), 0.5, 3.0, (), jnp.float32)
    down_weight = bell_draw(key_list[12], (FF, D), FF ** -0.5, 0.109375)
    second_gain = jnp.clip(1.0 + 0.18 * jax.random.normal(key_list[13], (D,), jnp.float32), 0.1, 1.9)
    second_shift = bell_draw(key_list[14], (D,), 0.5, 3.0, (), jnp.float32)
    project_weight = bell_draw(key_list[15], (D, PROJ), D ** -0.5, 0.21875)
    return dict(query_states=query_states, passage_states=passage_states, passage_bins=passage_bins, padding_mask=padding_mask, token_ids=token_ids, positives=positives, united_weight=united_weight, output_weight=output_weight, first_gain=first_gain, first_shift=first_shift, up_weight=up_weight, up_bias=up_bias, down_weight=down_weight, second_gain=second_gain, second_shift=second_shift, project_weight=project_weight)


SOFT_TEMP = 0.1
LOGIT_GAIN = 8.0
NORM_EPSILON = 1e-06
MASK_FILL = -1000000000.0
SCORE_SCALE = 0.125

@jax.custom_vjp
def low(v):
    return lax.optimization_barrier(v.astype(jnp.bfloat16)).astype(jnp.float32)

@jax.custom_vjp
def low_back(v):
    return v

def low_keep(v):
    return (low(v), None)

def low_pass(kept, grad):
    return (grad,)

def back_keep(v):
    return (v, None)

def back_low(kept, grad):
    return (low(grad),)
low.defvjp(low_keep, low_pass)
low_back.defvjp(back_keep, back_low)

def product(operand, partner):
    return jnp.dot(operand, partner, precision=lax.Precision.HIGHEST)

def layer_norm(hidden, gain_row, shift_row):
    centred = hidden - lax.optimization_barrier(jnp.mean(hidden, axis=-1, keepdims=True))
    spread = lax.optimization_barrier(jnp.mean(centred * centred, axis=-1, keepdims=True))
    return centred * lax.rsqrt(spread + NORM_EPSILON) * gain_row + shift_row

def attend(united_rows, allowed):
    row_count = united_rows.shape[0]
    stacked = united_rows.reshape(row_count, 3, HEADS, HEAD_DIM)
    raw_scores = jnp.einsum('qhd,khd->hqk', stacked[:, 0], stacked[:, 1], precision=lax.Precision.HIGHEST)
    scores = jnp.where(allowed[None], low_back(raw_scores * SCORE_SCALE), MASK_FILL)
    weights = low(jax.nn.softmax(scores, axis=-1))
    attended = jnp.einsum('hqk,khd->qhd', weights, stacked[:, 2], precision=lax.Precision.HIGHEST)
    return attended.reshape(row_count, D)

def query_attention(united_rows):
    grouped = united_rows.reshape(-1, QLEN, 3 * D)
    allowed = jnp.ones((QLEN, QLEN), dtype=jnp.bool_)

    def one_query(group_rows):
        return attend(group_rows, allowed)
    return jax.vmap(one_query)(grouped).reshape(-1, D)

def encode(rows_in, params, attention):
    united_weight, output_weight, first_gain, first_shift, up_weight, up_bias, down_weight, second_gain, second_shift, project_weight = params
    united_rows = low(low_back(product(rows_in, united_weight)))
    attended = low(low_back(attention(united_rows)))
    hidden_one = rows_in + low_back(product(attended, output_weight))
    norm_one = layer_norm(hidden_one, first_gain, first_shift)
    up_rows = low_back(product(low(norm_one), up_weight) + up_bias)
    active = low(jax.nn.gelu(up_rows, approximate=False))
    hidden_two = norm_one + low_back(product(active, down_weight))
    norm_two = layer_norm(hidden_two, second_gain, second_shift)
    projected = low_back(product(low(norm_two), project_weight))
    return low(projected * lax.rsqrt(lax.optimization_barrier(jnp.sum(projected * projected, axis=-1, keepdims=True)) + NORM_EPSILON))

def reference(query_states, passage_states, passage_bins, padding_mask, token_ids, positives, united_weight, output_weight, first_gain, first_shift, up_weight, up_bias, down_weight, second_gain, second_shift, project_weight):
    usable = (padding_mask == 1) & (token_ids >= SKIP_IDS)
    codes = jnp.where(usable, passage_bins, -1).astype(jnp.int32)
    slots = jnp.arange(PSG_DEV, dtype=jnp.int32)
    token_index = jnp.arange(PTOK_DEV, dtype=jnp.int32)
    diagonal = token_index[:, None] == token_index[None, :]

    def passage_attention(united_rows):
        blocks = united_rows.reshape(-1, PTOK_DEV, 3 * D)

        def one_block(packed):
            block_rows, bins_row, mask_row = packed
            allowed = (bins_row[:, None] == bins_row[None, :]) & ((mask_row[None, :] == 1) | diagonal)
            return attend(block_rows, allowed)
        return lax.map(jax.checkpoint(one_block), (blocks, passage_bins, padding_mask)).reshape(-1, D)

    def grid_logits(query_emb, passage_emb):

        def one_block(packed):
            emb_rows, code_row = packed
            similarity = low_back(product(query_emb, jnp.transpose(emb_rows)))
            member = (code_row[:, None] == slots[None, :]).astype(jnp.float32)
            bin_sums = product(jnp.exp(similarity / SOFT_TEMP), member)
            terms = SOFT_TEMP * jnp.log1p(bin_sums)
            return LOGIT_GAIN * lax.optimization_barrier(jnp.sum(terms.reshape(-1, QLEN, PSG_DEV), axis=1))
        blocks = lax.map(jax.checkpoint(one_block), (passage_emb.reshape(-1, PTOK_DEV, PROJ), codes))
        return jnp.transpose(blocks, (1, 0, 2)).reshape(blocks.shape[1], -1)

    def loss_of(query_rows, passage_rows, *params):
        query_emb = encode(query_rows, params, query_attention)
        passage_emb = encode(passage_rows, params, passage_attention)
        logits = grid_logits(query_emb, passage_emb)
        chosen = jnp.take_along_axis(logits, positives[:, None].astype(jnp.int32), axis=1)[:, 0]
        losses = jax.nn.logsumexp(logits, axis=1) - chosen
        return (jnp.sum(losses), (query_emb, passage_emb, losses))
    inputs = (query_states, passage_states, united_weight, output_weight, first_gain, first_shift, up_weight, up_bias, down_weight, second_gain, second_shift, project_weight)
    floats = tuple((member_array.astype(jnp.float32) for member_array in inputs))
    total_loss, pullback, extras = jax.vjp(loss_of, *floats, has_aux=True)
    grads = pullback(jnp.ones((), jnp.float32))
    return (extras[0].astype(jnp.bfloat16), extras[1].astype(jnp.bfloat16), extras[2], grads[0], grads[1], grads[2], grads[3], grads[4], grads[5], grads[6], grads[7], grads[8], grads[9], grads[10], grads[11])
```

```python
import jax
import jax.numpy as jnp
from jax import lax
from jax.experimental import pallas as pl
from jax.experimental.pallas import tpu as pltpu
from jax.sharding import PartitionSpec as P

D = 768
HEAD_DIM = 64
HEADS = 12
PROJ = 128
QLEN = 32
PSG_DEV = 4
SKIP_IDS = 3000
LANES = 128
TILE = 256


SOFT_TEMP = 0.1
LOGIT_GAIN = 8.0
NORM_EPSILON = 1e-06
MASK_FILL = -1000000000.0
SCORE_SCALE = 0.125


def layer_norm(hidden, gain_row, shift_row):
    centred = hidden - jnp.mean(hidden, axis=-1, keepdims=True)
    spread = jnp.mean(centred * centred, axis=-1, keepdims=True)
    return centred * lax.rsqrt(spread + NORM_EPSILON) * gain_row + shift_row


def unit_rows(projected):
    return projected * lax.rsqrt(
        jnp.sum(projected * projected, axis=-1, keepdims=True) + NORM_EPSILON
    )


def exact_gelu(inputs):
    return jax.nn.gelu(inputs, approximate=False)


def contract_rows(operand, partner):
    summed = jnp.einsum("rd,re->de", operand, partner, preferred_element_type=jnp.float32)
    return summed.astype(jnp.bfloat16)


def times_transposed(operand, partner):
    return jnp.einsum("re,de->rd", operand, partner, preferred_element_type=jnp.float32)


def split_heads(united_rows):
    stacked = united_rows.reshape(united_rows.shape[0], 3, HEADS, HEAD_DIM)
    return (stacked[:, 0], stacked[:, 1], stacked[:, 2])


def head_scores(head_query, head_key, allowed):
    raw_scores = (
        jnp.einsum("qhd,khd->hqk", head_query, head_key, preferred_element_type=jnp.float32)
        * SCORE_SCALE
    )
    return jnp.where(allowed[None], raw_scores, MASK_FILL)


def attend_forward(united_rows, allowed):
    head_query, head_key, head_value = split_heads(united_rows)
    scores = head_scores(head_query, head_key, allowed)
    row_peak = jnp.max(scores, axis=-1, keepdims=True)
    log_total = jnp.log(jnp.sum(jnp.exp(scores - row_peak), axis=-1, keepdims=True)) + row_peak
    weights = jnp.exp(scores - log_total).astype(jnp.bfloat16)
    attended = jnp.einsum("hqk,khd->qhd", weights, head_value, preferred_element_type=jnp.float32)
    return (attended.reshape(united_rows.shape[0], D).astype(jnp.bfloat16), log_total)


def attend_backward(united_rows, allowed, log_total, grad_attended):
    head_query, head_key, head_value = split_heads(united_rows)
    grad_heads = grad_attended.reshape(united_rows.shape[0], HEADS, HEAD_DIM)
    soft_weights = jnp.exp(head_scores(head_query, head_key, allowed) - log_total)
    weights_low = soft_weights.astype(jnp.bfloat16)
    grad_weights = jnp.einsum(
        "qhd,khd->hqk", grad_heads, head_value, preferred_element_type=jnp.float32
    )
    centre = jnp.sum(soft_weights * grad_weights, axis=-1, keepdims=True)
    grad_scores = (soft_weights * (grad_weights - centre)).astype(jnp.bfloat16)
    grad_query = (
        jnp.einsum("hqk,khd->qhd", grad_scores, head_key, preferred_element_type=jnp.float32)
        * SCORE_SCALE
    )
    grad_key = (
        jnp.einsum("hqk,qhd->khd", grad_scores, head_query, preferred_element_type=jnp.float32)
        * SCORE_SCALE
    )
    grad_value = jnp.einsum(
        "hqk,qhd->khd", weights_low, grad_heads, preferred_element_type=jnp.float32
    )
    joined = jnp.stack([grad_query, grad_key, grad_value], axis=1)
    return joined.reshape(united_rows.shape[0], 3 * D).astype(jnp.bfloat16)


def member_rows(code_row):
    slot_ids = lax.broadcasted_iota(jnp.int32, (LANES, code_row.shape[-1]), 0)
    return (code_row == slot_ids).astype(jnp.float32).astype(jnp.bfloat16)


def split_low(values):
    high = values.astype(jnp.bfloat16)
    return high, (values - high.astype(jnp.float32)).astype(jnp.bfloat16)


def exp_similarity(query_tile, passage_rows):
    similarity = lax.dot_general(
        query_tile, passage_rows, (((1,), (1,)), ((), ())), preferred_element_type=jnp.float32
    )
    return jnp.exp(similarity * (1.0 / SOFT_TEMP))


def tile_forward_kernel(query_ref, passage_ref, code_ref, inverse_ref, logit_ref):
    exp_sim = exp_similarity(query_ref[...], passage_ref[...])
    member = member_rows(code_ref[...])
    high, rest = split_low(exp_sim)
    contract = (((1,), (1,)), ((), ()))
    bin_sums = lax.dot_general(
        high, member, contract, preferred_element_type=jnp.float32
    ) + lax.dot_general(rest, member, contract, preferred_element_type=jnp.float32)
    inverse_ref[...] = 1.0 / (1.0 + bin_sums)
    terms = SOFT_TEMP * jnp.log1p(bin_sums)
    logit_ref[...] = LOGIT_GAIN * jnp.sum(terms.reshape(-1, QLEN, LANES), axis=1)


def tile_backward_kernel(
    query_ref, passage_ref, code_ref, inverse_ref, grad_ref, grad_query_ref, grad_passage_ref
):
    exp_sim = exp_similarity(query_ref[...], passage_ref[...])
    member = member_rows(code_ref[...])
    grad_tokens = LOGIT_GAIN * jnp.broadcast_to(
        grad_ref[...][:, None, :], (grad_ref.shape[0], QLEN, LANES)
    ).reshape(-1, LANES)
    high, rest = split_low(grad_tokens * inverse_ref[...])
    spread = jnp.dot(high, member, preferred_element_type=jnp.float32) + jnp.dot(
        rest, member, preferred_element_type=jnp.float32
    )
    grad_sim = (exp_sim * spread).astype(jnp.bfloat16)
    grad_query_ref[...] = jnp.dot(
        grad_sim, passage_ref[...], preferred_element_type=jnp.float32
    ).astype(jnp.bfloat16)
    partial = lax.dot_general(
        grad_sim, query_ref[...], (((0,), (0,)), ((), ())), preferred_element_type=jnp.float32
    )

    @pl.when(pl.program_id(0) == 0)
    def _():
        grad_passage_ref[...] = jnp.zeros_like(grad_passage_ref)

    grad_passage_ref[...] += partial


def tile_specs(token_count):
    rows = pl.BlockSpec((TILE, LANES), lambda i: (i, 0))
    fixed = pl.BlockSpec((token_count, PROJ), lambda i: (0, 0))
    codes = pl.BlockSpec((1, token_count), lambda i: (0, 0))
    few = pl.BlockSpec((TILE // QLEN, LANES), lambda i: (i, 0))
    return rows, fixed, codes, few


def tile_forward(queries, passages, codes):
    rows, fixed, code_spec, few = tile_specs(passages.shape[0])
    count = queries.shape[0]
    return pl.pallas_call(
        tile_forward_kernel,
        grid=(count // TILE,),
        in_specs=[rows, fixed, code_spec],
        out_specs=[rows, few],
        out_shape=[
            jax.ShapeDtypeStruct((count, LANES), jnp.float32),
            jax.ShapeDtypeStruct((count // QLEN, LANES), jnp.float32),
        ],
        name="tile_forward",
    )(queries, passages, codes)


def tile_backward(queries, passages, codes, inverse, grad_logits):
    rows, fixed, code_spec, few = tile_specs(passages.shape[0])
    count = queries.shape[0]
    return pl.pallas_call(
        tile_backward_kernel,
        grid=(count // TILE,),
        in_specs=[rows, fixed, code_spec, rows, few],
        out_specs=[rows, fixed],
        out_shape=[
            jax.ShapeDtypeStruct((count, PROJ), jnp.bfloat16),
            jax.ShapeDtypeStruct(passages.shape, jnp.float32),
        ],
        name="tile_backward",
    )(queries, passages, codes, inverse, grad_logits)


def add_low(first, second):
    return (first.astype(jnp.float32) + second.astype(jnp.float32)).astype(jnp.bfloat16)


def halved(part, axes, bit):
    place = axes.index(bit)
    mine = (lax.axis_index("pb") >> bit) & 1
    keep = lax.dynamic_index_in_dim(part, mine, place, False)
    send = lax.dynamic_index_in_dim(part, 1 - mine, place, False)
    pairs = [(i, i ^ (1 << bit)) for i in range(lax.axis_size("pb"))]
    return add_low(keep, lax.ppermute(send, "pb", pairs)), [a for a in axes if a != bit]


def scatter_sum(part):
    wide = lax.axis_size("pb")
    narrow = lax.axis_size("pa")
    bits = list(range(wide.bit_length() - 1))
    rows = part.shape[0] // (wide * narrow)
    columns = part.shape[1]
    part = part.reshape((2,) * len(bits) + (narrow, rows, columns))
    axes = bits[::-1]
    part, axes = halved(part, axes, 0)
    cut = columns // 2 // LANES * LANES
    pieces = [part[..., :cut], part[..., cut:]]
    orders = [bits[1:], bits[:0:-1]]
    done = []
    for piece, order in zip(pieces, orders):
        left = axes
        for bit in order:
            piece, left = halved(piece, left, bit)
        done.append(piece)
    joined = jnp.concatenate(done, axis=-1)
    mine = lax.axis_index("pa")
    total = lax.dynamic_index_in_dim(joined, mine, 0, False).astype(jnp.float32)
    for step in range(1, narrow):
        send = lax.dynamic_index_in_dim(joined, mine ^ step, 0, False)
        pairs = [(i, i ^ step) for i in range(narrow)]
        total = total + lax.ppermute(send, "pa", pairs).astype(jnp.float32)
    return total


def body(
    query_states,
    passage_states,
    passage_bins,
    padding_mask,
    token_ids,
    positives,
    united_weight,
    output_weight,
    first_gain,
    first_shift,
    up_weight,
    up_bias,
    down_weight,
    second_gain,
    second_shift,
    project_weight,
):
    query_count = query_states.shape[0]
    all_rows = jnp.concatenate([query_states, passage_states], axis=0)
    united_rows = jnp.dot(all_rows, united_weight, preferred_element_type=jnp.float32).astype(
        jnp.bfloat16
    )
    query_index = lax.broadcasted_iota(jnp.int32, (query_count, query_count), 0) // QLEN
    query_allowed = query_index == jnp.transpose(query_index)
    bins_row = passage_bins[0]
    mask_row = padding_mask[0]
    token_count = bins_row.shape[0]
    diagonal = lax.broadcasted_iota(
        jnp.int32, (token_count, token_count), 0
    ) == lax.broadcasted_iota(jnp.int32, (token_count, token_count), 1)
    passage_allowed = (bins_row[:, None] == bins_row[None, :]) & (
        (mask_row[None, :] == 1) | diagonal
    )
    query_attended, query_log_total = attend_forward(united_rows[:query_count], query_allowed)
    passage_attended, passage_log_total = attend_forward(united_rows[query_count:], passage_allowed)
    attended = jnp.concatenate([query_attended, passage_attended], axis=0)
    hidden_one = all_rows.astype(jnp.float32) + jnp.dot(
        attended, output_weight, preferred_element_type=jnp.float32
    )
    norm_one = layer_norm(hidden_one, first_gain, first_shift)
    norm_one_low = norm_one.astype(jnp.bfloat16)
    up_rows = jnp.dot(norm_one_low, up_weight, preferred_element_type=jnp.float32) + up_bias
    active_low = exact_gelu(up_rows).astype(jnp.bfloat16)
    hidden_two = norm_one + jnp.dot(active_low, down_weight, preferred_element_type=jnp.float32)
    norm_two = layer_norm(hidden_two, second_gain, second_shift)
    norm_two_low = norm_two.astype(jnp.bfloat16)
    projected = jnp.dot(norm_two_low, project_weight, preferred_element_type=jnp.float32)
    embedded = unit_rows(projected)
    embedded_low = embedded.astype(jnp.bfloat16)
    query_emb = embedded_low[:query_count]
    passage_emb = embedded_low[query_count:]
    usable = (mask_row == 1) & (token_ids[0] >= SKIP_IDS)
    own_codes = jnp.where(usable, bins_row, -1)
    own_index = lax.axis_index("pb") * lax.axis_size("pa") + lax.axis_index("pa")
    all_queries = lax.all_gather(query_emb, ("pb", "pa"), axis=0, tiled=True)
    code_row = own_codes[None, :]
    inverse, own_logits = tile_forward(all_queries, passage_emb, code_row)
    gathered = lax.all_gather(own_logits[:, :PSG_DEV], ("pb", "pa"), axis=0)
    row_peak = jnp.max(gathered, axis=(0, 2))
    log_norm = row_peak + jnp.log(
        jnp.sum(jnp.exp(gathered - row_peak[None, :, None]), axis=(0, 2))
    )
    shard_ids = lax.broadcasted_iota(jnp.int32, gathered.shape, 0)
    slot_ids = lax.broadcasted_iota(jnp.int32, gathered.shape, 2)
    hits = shard_ids * PSG_DEV + slot_ids == positives[None, :, None]
    losses = log_norm - jnp.sum(jnp.where(hits, gathered, 0.0), axis=(0, 2))
    queries_here = query_count // QLEN
    own_losses = lax.dynamic_slice_in_dim(losses, own_index * queries_here, queries_here)
    own_columns = own_index * PSG_DEV + lax.broadcasted_iota(jnp.int32, own_logits.shape, 1)
    grad_logits = jnp.exp(own_logits - log_norm[:, None]) - (
        own_columns == positives[:, None]
    ).astype(jnp.float32)
    all_grad, grad_passage_emb = tile_backward(
        all_queries, passage_emb, code_row, inverse, grad_logits
    )
    grad_query_emb = scatter_sum(all_grad)
    grad_embedded = jnp.concatenate([grad_query_emb, grad_passage_emb], axis=0)
    unit_pull = jax.vjp(unit_rows, projected)[1]
    grad_projected = unit_pull(grad_embedded)[0].astype(jnp.bfloat16)
    grad_project = contract_rows(norm_two_low, grad_projected)
    grad_norm_two = times_transposed(grad_projected, project_weight)
    second_pull = jax.vjp(layer_norm, hidden_two, second_gain, second_shift)[1]
    grad_hidden_two, grad_second_gain, grad_second_shift = second_pull(grad_norm_two)
    grad_branch_two = grad_hidden_two.astype(jnp.bfloat16)
    grad_down = contract_rows(active_low, grad_branch_two)
    grad_active = times_transposed(grad_branch_two, down_weight)
    gelu_pull = jax.vjp(exact_gelu, up_rows)[1]
    grad_up_rows = gelu_pull(grad_active)[0].astype(jnp.bfloat16)
    grad_up_bias = jnp.sum(grad_up_rows, axis=0, dtype=jnp.float32)
    grad_up = contract_rows(norm_one_low, grad_up_rows)
    grad_norm_one = times_transposed(grad_up_rows, up_weight) + grad_hidden_two
    first_pull = jax.vjp(layer_norm, hidden_one, first_gain, first_shift)[1]
    grad_hidden_one, grad_first_gain, grad_first_shift = first_pull(grad_norm_one)
    grad_branch_one = grad_hidden_one.astype(jnp.bfloat16)
    grad_output = contract_rows(attended, grad_branch_one)
    grad_attended = times_transposed(grad_branch_one, output_weight).astype(jnp.bfloat16)
    grad_query_united = attend_backward(
        united_rows[:query_count], query_allowed, query_log_total, grad_attended[:query_count]
    )
    grad_passage_united = attend_backward(
        united_rows[query_count:], passage_allowed, passage_log_total, grad_attended[query_count:]
    )
    grad_united_rows = jnp.concatenate([grad_query_united, grad_passage_united], axis=0)
    grad_united = contract_rows(all_rows, grad_united_rows)
    grad_rows = times_transposed(grad_united_rows, united_weight) + grad_hidden_one
    rows_in = D // (lax.axis_size("pb") * lax.axis_size("pa"))
    blocks = D // rows_in
    vectors = jnp.concatenate(
        [
            v.reshape(blocks, rows_in, -1)
            for v in (
                grad_first_gain, grad_first_shift, grad_second_gain, grad_second_shift, grad_up_bias
            )
        ],
        axis=-1,
    ).reshape(D, -1)
    vectors = jnp.pad(vectors, ((0, 0), (0, LANES - vectors.shape[1])))
    down_sum = scatter_sum(grad_down)
    up_sum = scatter_sum(grad_up)
    mixed = scatter_sum(
        jnp.concatenate([grad_output, grad_project, vectors.astype(jnp.bfloat16)], axis=1)
    )
    united_sum = scatter_sum(grad_united)
    small = mixed[:, D + PROJ :]
    shared = (
        united_sum,
        mixed[:, :D],
        small[:, 0],
        small[:, 1],
        up_sum,
        small[:, 4:8].reshape(-1),
        down_sum,
        small[:, 2],
        small[:, 3],
        mixed[:, D : D + PROJ],
    )
    return (
        query_emb,
        passage_emb,
        own_losses,
        grad_rows[:query_count],
        grad_rows[query_count:],
        shared[0],
        shared[1],
        shared[2],
        shared[3],
        shared[4],
        shared[5],
        shared[6],
        shared[7],
        shared[8],
        shared[9],
    )


def solution(mesh):
    return jax.shard_map(
        body,
        mesh=mesh,
        in_specs=(
            P(("pb", "pa"), None),
            P(("pb", "pa"), None),
            P(("pb", "pa"), None),
            P(("pb", "pa"), None),
            P(("pb", "pa"), None),
            P(),
            P(),
            P(),
            P(),
            P(),
            P(),
            P(),
            P(),
            P(),
            P(),
            P(),
        ),
        out_specs=(
            P(("pb", "pa"), None),
            P(("pb", "pa"), None),
            P(("pb", "pa")),
            P(("pb", "pa"), None),
            P(("pb", "pa"), None),
            P(("pb", "pa"), None),
            P(("pb", "pa"), None),
            P(("pb", "pa")),
            P(("pb", "pa")),
            P(("pb", "pa"), None),
            P(("pb", "pa")),
            P(("pb", "pa"), None),
            P(("pb", "pa")),
            P(("pb", "pa")),
            P(("pb", "pa"), None),
        ),
        check_vma=False,
    )
```

```python
import jax
import jax.numpy as jnp
from jax import lax
from jax.experimental import pallas as pl
from jax.experimental.pallas import tpu as pltpu
from jax.sharding import PartitionSpec as P

D = 768
HEAD_DIM = 64
HEADS = 12
PROJ = 128
QLEN = 32
PSG_DEV = 4
SKIP_IDS = 3000
LANES = 128
TILE = 256
ATTEND_TILE = 256
PAIRS = D // LANES


SOFT_TEMP = 0.1
LOGIT_GAIN = 8.0
NORM_EPSILON = 1e-06
MASK_FILL = -1000000000.0
SCORE_SCALE = 0.125


def layer_norm(hidden, gain_row, shift_row):
    centred = hidden - jnp.mean(hidden, axis=-1, keepdims=True)
    spread = jnp.mean(centred * centred, axis=-1, keepdims=True)
    return centred * lax.rsqrt(spread + NORM_EPSILON) * gain_row + shift_row


def unit_rows(projected):
    return projected * lax.rsqrt(
        jnp.sum(projected * projected, axis=-1, keepdims=True) + NORM_EPSILON
    )


def exact_gelu(inputs):
    return jax.nn.gelu(inputs, approximate=False)


def contract_rows(operand, partner):
    summed = jnp.einsum("rd,re->de", operand, partner, preferred_element_type=jnp.float32)
    return summed.astype(jnp.bfloat16)


def times_transposed(operand, partner):
    return jnp.einsum("re,de->rd", operand, partner, preferred_element_type=jnp.float32)


def head_part(values, head):
    lane = lax.broadcasted_iota(jnp.int32, values.shape, 1)
    return jnp.where(lane // HEAD_DIM == head, values, jnp.zeros_like(values))


def mul_nt(operand, partner):
    return lax.dot_general(
        operand, partner, (((1,), (1,)), ((), ())), preferred_element_type=jnp.float32
    )


def mul_tn(operand, partner):
    return lax.dot_general(
        operand, partner, (((0,), (0,)), ((), ())), preferred_element_type=jnp.float32
    )


def mul_nn(operand, partner):
    return jnp.dot(operand, partner, preferred_element_type=jnp.float32)


def write_bias(bias_ref, bin_column_ref, bin_row_ref, mask_column_ref):
    @pl.when(pl.program_id(0) == 0)
    def _():
        keys = lax.broadcasted_iota(jnp.int32, bias_ref.shape, 0)
        queries = lax.broadcasted_iota(jnp.int32, bias_ref.shape, 1)
        allowed = (bin_column_ref[...] == bin_row_ref[...]) & (
            (mask_column_ref[...] == 1) | (keys == queries)
        )
        bias_ref[...] = jnp.where(allowed, 0.0, MASK_FILL)


def query_bias(count):
    keys = lax.broadcasted_iota(jnp.int32, (count, count), 0) // QLEN
    queries = lax.broadcasted_iota(jnp.int32, (count, count), 1) // QLEN
    return jnp.where(keys == queries, 0.0, MASK_FILL)


def attend_forward_kernel(
    q_ref, k_ref, v_ref, bin_column_ref, bin_row_ref, mask_column_ref, out_ref, log_ref, bias_ref
):
    write_bias(bias_ref, bin_column_ref, bin_row_ref, mask_column_ref)
    tokens = bias_ref.shape[0]
    rows = q_ref.shape[0]

    def block(low, high, key_low, key_high, bias):
        query = q_ref[low:high, :] * SCORE_SCALE
        key = k_ref[key_low:key_high, :]
        value = v_ref[key_low:key_high, :]
        out = None
        for head in range(2):
            scores = mul_nt(head_part(key, head), query) + bias
            peak = jnp.max(scores, axis=0, keepdims=True)
            raised = jnp.exp(scores - peak)
            total = jnp.sum(raised, axis=0, keepdims=True)
            log_ref[0, head : head + 1, low:high] = peak + jnp.log(total)
            weights = (raised * (1.0 / total)).astype(jnp.bfloat16)
            part = mul_tn(weights, head_part(value, head))
            out = part if out is None else out + part
        out_ref[low:high, :] = out.astype(jnp.bfloat16)

    block(tokens, rows, tokens, rows, query_bias(rows - tokens))
    for low in range(0, tokens, ATTEND_TILE):
        high = low + ATTEND_TILE
        block(low, high, 0, tokens, bias_ref[:, low:high])


def attend_backward_kernel(
    q_ref,
    k_ref,
    v_ref,
    grad_ref,
    bin_column_ref,
    bin_row_ref,
    mask_column_ref,
    log_ref,
    out_ref,
    bias_ref,
    grad_key_ref,
    grad_value_ref,
):
    write_bias(bias_ref, bin_column_ref, bin_row_ref, mask_column_ref)
    tokens = bias_ref.shape[0]
    rows = q_ref.shape[0]
    width = out_ref.shape[1] // 3
    base = pl.program_id(0) * LANES
    columns = [pl.ds(pl.multiple_of(base + i * width, LANES), LANES) for i in range(3)]

    def block(low, high, key_low, key_high, bias):
        query = q_ref[low:high, :] * SCORE_SCALE
        grad = grad_ref[low:high, :]
        key = k_ref[key_low:key_high, :]
        value = v_ref[key_low:key_high, :]
        sums = None
        for head in range(2):
            own_key = head_part(key, head)
            scores = mul_nt(own_key, query) + bias
            weights = jnp.exp(scores - log_ref[0, head : head + 1, low:high])
            weighted = weights * mul_nt(head_part(value, head), grad)
            centre = jnp.sum(weighted, axis=0, keepdims=True)
            grad_scores = (weighted - weights * centre).astype(jnp.bfloat16)
            parts = (
                mul_tn(grad_scores, own_key),
                mul_nn(grad_scores, head_part(query, head)),
                mul_nn(weights.astype(jnp.bfloat16), head_part(grad, head)),
            )
            sums = parts if sums is None else tuple(a + b for a, b in zip(sums, parts))
        out_ref[low:high, columns[0]] = (sums[0] * SCORE_SCALE).astype(jnp.bfloat16)
        return sums[1:]

    grad_key, grad_value = block(tokens, rows, tokens, rows, query_bias(rows - tokens))
    out_ref[tokens:, columns[1]] = grad_key.astype(jnp.bfloat16)
    out_ref[tokens:, columns[2]] = grad_value.astype(jnp.bfloat16)
    for low in range(0, tokens, ATTEND_TILE):
        high = low + ATTEND_TILE
        grad_key, grad_value = block(low, high, 0, tokens, bias_ref[:, low:high])
        if low == 0:
            grad_key_ref[...] = grad_key
            grad_value_ref[...] = grad_value
        else:
            grad_key_ref[...] += grad_key
            grad_value_ref[...] += grad_value
    out_ref[:tokens, columns[1]] = grad_key_ref[...].astype(jnp.bfloat16)
    out_ref[:tokens, columns[2]] = grad_value_ref[...].astype(jnp.bfloat16)


def fixed_block(shape):
    return pl.BlockSpec(shape, lambda i: (0,) * len(shape))


def attend_specs(rows, tokens, first):
    def pair_block(part):
        return pl.BlockSpec((rows, LANES), lambda i: (0, part * PAIRS + first + i))

    specs = [pair_block(0), pair_block(1), pair_block(2)]
    masks = [fixed_block((tokens, 1)), fixed_block((1, tokens)), fixed_block((tokens, 1))]
    logs = pl.BlockSpec((1, 2, rows), lambda i: (first + i, 0, 0))
    return specs, masks, logs


def attend_forward(united_rows, masks):
    rows = united_rows.shape[0]
    tokens = masks[0].shape[0]
    specs, mask_specs, logs = attend_specs(rows, tokens, 0)
    return pl.pallas_call(
        attend_forward_kernel,
        grid=(PAIRS,),
        in_specs=specs + mask_specs,
        out_specs=[specs[0], logs],
        out_shape=[
            jax.ShapeDtypeStruct((rows, D), jnp.bfloat16),
            jax.ShapeDtypeStruct((PAIRS, 2, rows), jnp.float32),
        ],
        scratch_shapes=[pltpu.VMEM((tokens, tokens), jnp.float32)],
        name="attend_forward",
    )(united_rows, united_rows, united_rows, *masks)


def attend_backward(united_rows, grad_attended, masks, logs, first, count):
    rows = united_rows.shape[0]
    tokens = masks[0].shape[0]
    specs, mask_specs, log_spec = attend_specs(rows, tokens, first)
    width = 3 * count * LANES
    return pl.pallas_call(
        attend_backward_kernel,
        grid=(count,),
        in_specs=specs + [specs[0]] + mask_specs + [log_spec],
        out_specs=fixed_block((rows, width)),
        out_shape=jax.ShapeDtypeStruct((rows, width), jnp.bfloat16),
        scratch_shapes=[
            pltpu.VMEM((tokens, tokens), jnp.float32),
            pltpu.VMEM((tokens, LANES), jnp.float32),
            pltpu.VMEM((tokens, LANES), jnp.float32),
        ],
        name="attend_backward",
    )(united_rows, united_rows, united_rows, grad_attended, *masks, logs)


def member_rows(code_row):
    slot_ids = lax.broadcasted_iota(jnp.int32, (LANES, code_row.shape[-1]), 0)
    return (code_row == slot_ids).astype(jnp.float32).astype(jnp.bfloat16)


def split_low(values):
    high = values.astype(jnp.bfloat16)
    return high, (values - high.astype(jnp.float32)).astype(jnp.bfloat16)


def exp_similarity(query_tile, passage_rows):
    similarity = lax.dot_general(
        query_tile, passage_rows, (((1,), (1,)), ((), ())), preferred_element_type=jnp.float32
    )
    return jnp.exp(similarity * (1.0 / SOFT_TEMP))


def order_matrix(order_ref):
    count = order_ref.shape[0]
    return (order_ref[...] == lax.broadcasted_iota(jnp.int32, (count, count), 1)).astype(
        jnp.float32
    )


def own_hits(own_ref, positive_ref, rows):
    shape = (rows, positive_ref.shape[1])
    row = lax.broadcasted_iota(jnp.int32, shape, 0)
    hit = (own_ref[0] * PSG_DEV + row == positive_ref[...]) & (row < PSG_DEV)
    return row, hit.astype(jnp.float32)


def tile_forward_kernel(
    own_ref,
    query_ref,
    passage_ref,
    code_ref,
    order_ref,
    positive_ref,
    inverse_ref,
    logit_ref,
    rows_ref,
):
    step = pl.program_id(0)
    exp_sim = exp_similarity(query_ref[...], passage_ref[...])
    member = member_rows(code_ref[...])
    high, rest = split_low(exp_sim)
    bin_sums = mul_nt(high, member) + mul_nt(rest, member)
    inverse_ref[...] = 1.0 / (1.0 + bin_sums)
    terms = SOFT_TEMP * jnp.log1p(bin_sums)
    few = TILE // QLEN
    rows_ref[pl.ds(pl.multiple_of(step * few, few), few), :] = LOGIT_GAIN * jnp.sum(
        terms.reshape(-1, QLEN, LANES), axis=1
    )

    @pl.when(step == pl.num_programs(0) - 1)
    def _():
        logits = lax.dot_general(
            rows_ref[...],
            order_matrix(order_ref),
            (((0,), (0,)), ((), ())),
            precision=lax.Precision.HIGHEST,
            preferred_element_type=jnp.float32,
        )[: 2 * PSG_DEV, :]
        row, hit = own_hits(own_ref, positive_ref, 2 * PSG_DEV)
        chosen = jnp.sum(logits * hit, axis=0, keepdims=True)
        logit_ref[0] = jnp.where(row == PSG_DEV, chosen, logits)


def tile_backward_kernel(
    own_ref,
    query_ref,
    passage_ref,
    code_ref,
    order_ref,
    positive_ref,
    inverse_ref,
    own_logit_ref,
    logit_ref,
    grad_query_ref,
    grad_passage_ref,
    loss_ref,
    rows_ref,
):
    step = pl.program_id(0)

    @pl.when(step == 0)
    def _():
        grad_passage_ref[...] = jnp.zeros_like(grad_passage_ref)
        logits = logit_ref[:, :PSG_DEV, :]
        peak = jnp.max(jnp.max(logits, axis=0), axis=0, keepdims=True)
        raised = jnp.exp(logits - peak[None])
        log_norm = peak + jnp.log(jnp.sum(jnp.sum(raised, axis=0), axis=0, keepdims=True))
        loss_ref[...] = log_norm - jnp.sum(logit_ref[:, PSG_DEV, :], axis=0, keepdims=True)
        row, hit = own_hits(own_ref, positive_ref, 2 * PSG_DEV)
        grads = jnp.where(row < PSG_DEV, jnp.exp(own_logit_ref[0] - log_norm) - hit, 0.0)
        grads = jnp.concatenate(
            [grads, jnp.zeros((LANES - 2 * PSG_DEV, grads.shape[1]), jnp.float32)], axis=0
        )
        rows_ref[...] = LOGIT_GAIN * lax.dot_general(
            order_matrix(order_ref),
            grads,
            (((1,), (1,)), ((), ())),
            precision=lax.Precision.HIGHEST,
            preferred_element_type=jnp.float32,
        )

    exp_sim = exp_similarity(query_ref[...], passage_ref[...])
    member = member_rows(code_ref[...])
    few = TILE // QLEN
    grad_rows = rows_ref[pl.ds(pl.multiple_of(step * few, few), few), :]
    grad_tokens = jnp.broadcast_to(grad_rows[:, None, :], (few, QLEN, LANES)).reshape(-1, LANES)
    high, rest = split_low(grad_tokens * inverse_ref[...])
    spread = mul_nn(high, member) + mul_nn(rest, member)
    grad_sim = (exp_sim * spread).astype(jnp.bfloat16)
    grad_query_ref[...] = mul_nn(grad_sim, passage_ref[...])
    grad_passage_ref[...] += mul_tn(grad_sim, query_ref[...])


def tile_forward(own, queries, passages, codes, order, positives):
    count = queries.shape[0]
    tokens = passages.shape[0]
    rows = pl.BlockSpec((TILE, LANES), lambda i: (i, 0))
    found = order.shape[0]
    return pl.pallas_call(
        tile_forward_kernel,
        grid=(count // TILE,),
        in_specs=[
            pl.BlockSpec(memory_space=pltpu.SMEM),
            rows,
            fixed_block((tokens, PROJ)),
            fixed_block((1, tokens)),
            fixed_block((found, 1)),
            fixed_block((1, found)),
        ],
        out_specs=[rows, fixed_block((1, 2 * PSG_DEV, found))],
        out_shape=[
            jax.ShapeDtypeStruct((count, LANES), jnp.float32),
            jax.ShapeDtypeStruct((1, 2 * PSG_DEV, found), jnp.float32),
        ],
        scratch_shapes=[pltpu.VMEM((found, LANES), jnp.float32)],
        name="tile_forward",
    )(own, queries, passages, codes, order, positives)


def tile_backward(own, queries, passages, codes, order, positives, inverse, own_logits, logits):
    count = queries.shape[0]
    tokens = passages.shape[0]
    rows = pl.BlockSpec((TILE, LANES), lambda i: (i, 0))
    found = order.shape[0]
    return pl.pallas_call(
        tile_backward_kernel,
        grid=(count // TILE,),
        in_specs=[
            pl.BlockSpec(memory_space=pltpu.SMEM),
            rows,
            fixed_block((tokens, PROJ)),
            fixed_block((1, tokens)),
            fixed_block((found, 1)),
            fixed_block((1, found)),
            rows,
            fixed_block(own_logits.shape),
            fixed_block(logits.shape),
        ],
        out_specs=[rows, fixed_block((tokens, PROJ)), fixed_block((1, found))],
        out_shape=[
            jax.ShapeDtypeStruct((count, PROJ), jnp.float32),
            jax.ShapeDtypeStruct(passages.shape, jnp.float32),
            jax.ShapeDtypeStruct((1, found), jnp.float32),
        ],
        scratch_shapes=[pltpu.VMEM((found, LANES), jnp.float32)],
        name="tile_backward",
    )(own, queries, passages, codes, order, positives, inverse, own_logits, logits)


def swap_wide(part, bit):
    pairs = [(i, i ^ (1 << bit)) for i in range(lax.axis_size("pb"))]
    return lax.ppermute(part, "pb", pairs)


def swap_narrow(part, step):
    pairs = [(i, i ^ step) for i in range(lax.axis_size("pa"))]
    return lax.ppermute(part, "pa", pairs)


def wide_bits():
    count = lax.axis_size("pb").bit_length() - 1
    return list(range(1, count)) + [0]


def relative_masks():
    narrow = lax.axis_size("pa")
    masks = list(range(narrow))
    for bit in wide_bits():
        masks = masks + [m ^ (narrow << bit) for m in masks]
    return masks


def gather_relative(part):
    parts = [part] + [swap_narrow(part, s) for s in range(1, lax.axis_size("pa"))]
    whole = jnp.concatenate(parts, axis=0)
    for bit in wide_bits():
        whole = jnp.concatenate([whole, swap_wide(whole, bit)], axis=0)
    return whole


def sum_relative(whole):
    for bit in wide_bits()[::-1]:
        half = whole.shape[0] // 2
        whole = whole[:half] + swap_wide(whole[half:], bit)
    narrow = lax.axis_size("pa")
    size = whole.shape[0] // narrow
    total = whole[:size]
    for step in range(1, narrow):
        total = total + swap_narrow(whole[step * size : (step + 1) * size], step)
    return total


def add_low(first, second):
    return (first.astype(jnp.float32) + second.astype(jnp.float32)).astype(jnp.bfloat16)


class ScatterSum:
    def __init__(self, part):
        wide = lax.axis_size("pb")
        narrow = lax.axis_size("pa")
        bits = list(range(wide.bit_length() - 1))
        self.columns = part.shape[1]
        self.rows = part.shape[0] // (wide * narrow)
        part = part.reshape((2,) * len(bits) + (narrow, self.rows, self.columns))
        self.axes = [bits[::-1]]
        self.kept = []
        self.flight = []
        self.total = None
        self.orders = [bits[:1]]
        self.later = [bits[1:], bits[:0:-1]]
        self.launch([part])

    def launch(self, pieces):
        self.kept, self.flight = [], []
        for i, piece in enumerate(pieces):
            bit = self.orders[i][0]
            place = self.axes[i].index(bit)
            mine = (lax.axis_index("pb") >> bit) & 1
            self.kept.append(lax.dynamic_index_in_dim(piece, mine, place, False))
            send = lax.dynamic_index_in_dim(piece, 1 - mine, place, False)
            self.flight.append(swap_wide(send, bit))
            self.axes[i] = [a for a in self.axes[i] if a != bit]
        self.orders = [order[1:] for order in self.orders]

    def advance(self):
        if self.total is not None:
            return
        if self.orders is None:
            self.total = self.kept[0]
            for part in self.flight:
                self.total = self.total + part.astype(jnp.float32)
            self.flight = []
            return
        pieces = [add_low(a, b) for a, b in zip(self.kept, self.flight)]
        if not self.orders[0] and self.later is not None:
            cut = self.columns // 2 // LANES * LANES
            pieces = [pieces[0][..., :cut], pieces[0][..., cut:]]
            self.axes = [self.axes[0], self.axes[0]]
            self.orders, self.later = self.later, None
        if self.orders[0]:
            self.launch(pieces)
            return
        joined = jnp.concatenate(pieces, axis=-1)
        mine = lax.axis_index("pa")
        self.kept = [lax.dynamic_index_in_dim(joined, mine, 0, False).astype(jnp.float32)]
        self.flight = [
            swap_narrow(lax.dynamic_index_in_dim(joined, mine ^ step, 0, False), step)
            for step in range(1, lax.axis_size("pa"))
        ]
        self.orders = None

    def finish(self):
        while self.total is None:
            self.advance()
        return self.total


def meet(chain, sums):
    flights = [s.flight for s in sums]
    chain, flights = lax.optimization_barrier((chain, flights))
    for one, flight in zip(sums, flights):
        one.flight = flight
        one.advance()
    return chain


def body(
    query_states,
    passage_states,
    passage_bins,
    padding_mask,
    token_ids,
    positives,
    united_weight,
    output_weight,
    first_gain,
    first_shift,
    up_weight,
    up_bias,
    down_weight,
    second_gain,
    second_shift,
    project_weight,
):
    query_count = query_states.shape[0]
    token_count = passage_states.shape[0]
    all_rows = jnp.concatenate([passage_states, query_states], axis=0)
    united_rows = jnp.dot(all_rows, united_weight, preferred_element_type=jnp.float32).astype(
        jnp.bfloat16
    )
    bins_row = passage_bins[0]
    mask_row = padding_mask[0]
    masks = (bins_row[:, None], passage_bins, mask_row[:, None])
    attended, logs = attend_forward(united_rows, masks)
    hidden_one = all_rows.astype(jnp.float32) + jnp.dot(
        attended, output_weight, preferred_element_type=jnp.float32
    )
    norm_one = layer_norm(hidden_one, first_gain, first_shift)
    norm_one_low = norm_one.astype(jnp.bfloat16)
    up_rows = jnp.dot(norm_one_low, up_weight, preferred_element_type=jnp.float32) + up_bias
    active_low = exact_gelu(up_rows).astype(jnp.bfloat16)
    hidden_two = norm_one + jnp.dot(active_low, down_weight, preferred_element_type=jnp.float32)
    norm_two = layer_norm(hidden_two, second_gain, second_shift)
    norm_two_low = norm_two.astype(jnp.bfloat16)
    projected = jnp.dot(norm_two_low, project_weight, preferred_element_type=jnp.float32)
    embedded = unit_rows(projected)
    embedded_low = embedded.astype(jnp.bfloat16)
    query_emb = embedded_low[token_count:]
    passage_emb = embedded_low[:token_count]
    usable = (mask_row == 1) & (token_ids[0] >= SKIP_IDS)
    own_codes = jnp.where(usable, bins_row, -1)
    own_index = lax.axis_index("pb") * lax.axis_size("pa") + lax.axis_index("pa")
    own = own_index.reshape(1)
    queries_here = query_count // QLEN
    blocks = own_index ^ jnp.array(relative_masks(), jnp.int32)
    order = (
        blocks[:, None] * queries_here + lax.broadcasted_iota(jnp.int32, (1, queries_here), 1)
    ).reshape(-1, 1)
    all_queries = gather_relative(query_emb)
    code_row = own_codes[None, :]
    wanted = positives[None, :]
    inverse, own_logits = tile_forward(own, all_queries, passage_emb, code_row, order, wanted)
    logits = gather_relative(own_logits)
    all_grad, grad_passage_emb, losses = tile_backward(
        own, all_queries, passage_emb, code_row, order, wanted, inverse, own_logits, logits
    )
    own_losses = lax.dynamic_slice_in_dim(losses[0], own_index * queries_here, queries_here)
    grad_query_emb = sum_relative(all_grad)
    grad_embedded = jnp.concatenate([grad_passage_emb, grad_query_emb], axis=0)
    unit_pull = jax.vjp(unit_rows, projected)[1]
    grad_projected = unit_pull(grad_embedded)[0].astype(jnp.bfloat16)
    grad_project = contract_rows(norm_two_low, grad_projected)
    grad_norm_two = times_transposed(grad_projected, project_weight)
    second_pull = jax.vjp(layer_norm, hidden_two, second_gain, second_shift)[1]
    grad_hidden_two, grad_second_gain, grad_second_shift = second_pull(grad_norm_two)
    grad_branch_two = grad_hidden_two.astype(jnp.bfloat16)
    down_sum = ScatterSum(contract_rows(active_low, grad_branch_two))
    grad_active = times_transposed(grad_branch_two, down_weight)
    gelu_pull = jax.vjp(exact_gelu, up_rows)[1]
    grad_up_rows = gelu_pull(grad_active)[0].astype(jnp.bfloat16)
    grad_up_rows = meet(grad_up_rows, [down_sum])
    grad_up_bias = jnp.sum(grad_up_rows, axis=0, dtype=jnp.float32)
    up_sum = ScatterSum(contract_rows(norm_one_low, grad_up_rows))
    grad_norm_one = times_transposed(grad_up_rows, up_weight) + grad_hidden_two
    first_pull = jax.vjp(layer_norm, hidden_one, first_gain, first_shift)[1]
    grad_hidden_one, grad_first_gain, grad_first_shift = first_pull(grad_norm_one)
    grad_branch_one = grad_hidden_one.astype(jnp.bfloat16)
    grad_branch_one = meet(grad_branch_one, [down_sum, up_sum])
    grad_output = contract_rows(attended, grad_branch_one)
    devices = lax.axis_size("pb") * lax.axis_size("pa")
    vectors = jnp.concatenate(
        [
            v.reshape(devices, D // devices, -1)
            for v in (
                grad_first_gain, grad_first_shift, grad_second_gain, grad_second_shift, grad_up_bias
            )
        ],
        axis=-1,
    ).reshape(D, -1)
    vectors = jnp.pad(vectors, ((0, 0), (0, LANES - vectors.shape[1]))).astype(jnp.bfloat16)
    mixed_sum = ScatterSum(jnp.concatenate([grad_output, grad_project, vectors], axis=1))
    grad_attended = times_transposed(grad_branch_one, output_weight).astype(jnp.bfloat16)
    grad_united = []
    united_sums = []
    running = [down_sum, up_sum, mixed_sum]
    width = PAIRS // 2
    for first in range(0, PAIRS, width):
        grad_part = attend_backward(united_rows, grad_attended, masks, logs, first, width)
        grad_part, grad_attended = meet((grad_part, grad_attended), running + united_sums)
        united_sums.append(ScatterSum(contract_rows(all_rows, grad_part)))
        grad_united.append(grad_part)
    step = width * LANES

    def joined(parts):
        pieces = [p[:, i * step : (i + 1) * step] for i in range(3) for p in parts]
        return jnp.concatenate(pieces, axis=1)

    grad_united_rows = joined(grad_united)
    grad_rows = times_transposed(grad_united_rows, united_weight) + grad_hidden_one
    down_total = down_sum.finish()
    up_total = up_sum.finish()
    mixed = mixed_sum.finish()
    united_total = joined([one.finish() for one in united_sums])
    small = mixed[:, D + PROJ :]
    shared = (
        united_total,
        mixed[:, :D],
        small[:, 0],
        small[:, 1],
        up_total,
        small[:, 4:8].reshape(-1),
        down_total,
        small[:, 2],
        small[:, 3],
        mixed[:, D : D + PROJ],
    )
    return (
        query_emb,
        passage_emb,
        own_losses,
        grad_rows[token_count:],
        grad_rows[:token_count],
        shared[0],
        shared[1],
        shared[2],
        shared[3],
        shared[4],
        shared[5],
        shared[6],
        shared[7],
        shared[8],
        shared[9],
    )


def solution(mesh):
    return jax.shard_map(
        body,
        mesh=mesh,
        in_specs=(
            P(("pb", "pa"), None),
            P(("pb", "pa"), None),
            P(("pb", "pa"), None),
            P(("pb", "pa"), None),
            P(("pb", "pa"), None),
            P(),
            P(),
            P(),
            P(),
            P(),
            P(),
            P(),
            P(),
            P(),
            P(),
            P(),
        ),
        out_specs=(
            P(("pb", "pa"), None),
            P(("pb", "pa"), None),
            P(("pb", "pa")),
            P(("pb", "pa"), None),
            P(("pb", "pa"), None),
            P(("pb", "pa"), None),
            P(("pb", "pa"), None),
            P(("pb", "pa")),
            P(("pb", "pa")),
            P(("pb", "pa"), None),
            P(("pb", "pa")),
            P(("pb", "pa"), None),
            P(("pb", "pa")),
            P(("pb", "pa")),
            P(("pb", "pa"), None),
        ),
        check_vma=False,
    )
```

```python
import functools

import jax
import jax.numpy as jnp
from jax import lax
from jax.experimental import pallas as pl
from jax.experimental.pallas import tpu as pltpu
from jax.sharding import PartitionSpec as P

D = 768
HEAD_DIM = 64
HEADS = 12
PROJ = 128
QLEN = 32
PSG_DEV = 4
SKIP_IDS = 3000
LANES = 128
TILE = 256
ATTEND_TILE = 256
PAIRS = D // LANES
GELU_TILE = 512
GELU_PARTS = 4
TAIL_RATE = 0.23
TAIL_TERMS = (
    -2.7766233e-05,
    0.09237861,
    0.08576121,
    0.119523115,
    -0.03294691,
    0.3015191,
    -0.27817392,
    0.29043987,
    -0.07847336,
)
BELL_SCALE = 0.3989422804014327


SOFT_TEMP = 0.1
LOGIT_GAIN = 8.0
NORM_EPSILON = 1e-06
MASK_FILL = -1000000000.0
SCORE_SCALE = 0.125


def layer_norm(hidden, gain_row, shift_row):
    centred = hidden - jnp.mean(hidden, axis=-1, keepdims=True)
    spread = jnp.mean(centred * centred, axis=-1, keepdims=True)
    return centred * lax.rsqrt(spread + NORM_EPSILON) * gain_row + shift_row


def unit_rows(projected):
    return projected * lax.rsqrt(
        jnp.sum(projected * projected, axis=-1, keepdims=True) + NORM_EPSILON
    )


def contract_rows(operand, partner):
    summed = jnp.einsum("rd,re->de", operand, partner, preferred_element_type=jnp.float32)
    return summed.astype(jnp.bfloat16)


def times_transposed(operand, partner):
    return jnp.einsum("re,de->rd", operand, partner, preferred_element_type=jnp.float32)


def head_part(values, head):
    lane = lax.broadcasted_iota(jnp.int32, values.shape, 1)
    return jnp.where(lane // HEAD_DIM == head, values, jnp.zeros_like(values))


def mul_nt(operand, partner):
    return lax.dot_general(
        operand, partner, (((1,), (1,)), ((), ())), preferred_element_type=jnp.float32
    )


def mul_tn(operand, partner):
    return lax.dot_general(
        operand, partner, (((0,), (0,)), ((), ())), preferred_element_type=jnp.float32
    )


def mul_nn(operand, partner):
    return jnp.dot(operand, partner, preferred_element_type=jnp.float32)


def write_bias(bias_ref, bin_column_ref, bin_row_ref, mask_column_ref):
    @pl.when(pl.program_id(0) == 0)
    def _():
        keys = lax.broadcasted_iota(jnp.int32, bias_ref.shape, 0)
        queries = lax.broadcasted_iota(jnp.int32, bias_ref.shape, 1)
        allowed = (bin_column_ref[...] == bin_row_ref[...]) & (
            (mask_column_ref[...] == 1) | (keys == queries)
        )
        bias_ref[...] = jnp.where(allowed, 0.0, MASK_FILL)


def query_bias(count):
    keys = lax.broadcasted_iota(jnp.int32, (count, count), 0) // QLEN
    queries = lax.broadcasted_iota(jnp.int32, (count, count), 1) // QLEN
    return jnp.where(keys == queries, 0.0, MASK_FILL)


def attend_forward_kernel(
    q_ref, k_ref, v_ref, bin_column_ref, bin_row_ref, mask_column_ref, out_ref, log_ref, bias_ref
):
    write_bias(bias_ref, bin_column_ref, bin_row_ref, mask_column_ref)
    tokens = bias_ref.shape[0]
    rows = q_ref.shape[0]

    def block(low, high, key_low, key_high, bias):
        query = q_ref[low:high, :] * SCORE_SCALE
        key = k_ref[key_low:key_high, :]
        value = v_ref[key_low:key_high, :]
        out = None
        for head in range(2):
            scores = mul_nt(head_part(key, head), query) + bias
            peak = jnp.max(scores, axis=0, keepdims=True)
            raised = jnp.exp(scores - peak)
            total = jnp.sum(raised, axis=0, keepdims=True)
            log_ref[0, head : head + 1, low:high] = peak + jnp.log(total)
            weights = (raised * (1.0 / total)).astype(jnp.bfloat16)
            part = mul_tn(weights, head_part(value, head))
            out = part if out is None else out + part
        out_ref[low:high, :] = out.astype(jnp.bfloat16)

    block(tokens, rows, tokens, rows, query_bias(rows - tokens))
    for low in range(0, tokens, ATTEND_TILE):
        high = low + ATTEND_TILE
        block(low, high, 0, tokens, bias_ref[:, low:high])


def attend_backward_kernel(
    q_ref,
    k_ref,
    v_ref,
    grad_ref,
    bin_column_ref,
    bin_row_ref,
    mask_column_ref,
    log_ref,
    out_ref,
    bias_ref,
    grad_key_ref,
    grad_value_ref,
):
    write_bias(bias_ref, bin_column_ref, bin_row_ref, mask_column_ref)
    tokens = bias_ref.shape[0]
    rows = q_ref.shape[0]
    width = out_ref.shape[1] // 3
    base = pl.program_id(0) * LANES
    columns = [pl.ds(pl.multiple_of(base + i * width, LANES), LANES) for i in range(3)]

    def block(low, high, key_low, key_high, bias):
        query = q_ref[low:high, :] * SCORE_SCALE
        grad = grad_ref[low:high, :]
        key = k_ref[key_low:key_high, :]
        value = v_ref[key_low:key_high, :]
        sums = None
        for head in range(2):
            own_key = head_part(key, head)
            scores = mul_nt(own_key, query) + bias
            weights = jnp.exp(scores - log_ref[0, head : head + 1, low:high])
            weighted = weights * mul_nt(head_part(value, head), grad)
            centre = jnp.sum(weighted, axis=0, keepdims=True)
            grad_scores = (weighted - weights * centre).astype(jnp.bfloat16)
            parts = (
                mul_tn(grad_scores, own_key),
                mul_nn(grad_scores, head_part(query, head)),
                mul_nn(weights.astype(jnp.bfloat16), head_part(grad, head)),
            )
            sums = parts if sums is None else tuple(a + b for a, b in zip(sums, parts))
        out_ref[low:high, columns[0]] = (sums[0] * SCORE_SCALE).astype(jnp.bfloat16)
        return sums[1:]

    grad_key, grad_value = block(tokens, rows, tokens, rows, query_bias(rows - tokens))
    out_ref[tokens:, columns[1]] = grad_key.astype(jnp.bfloat16)
    out_ref[tokens:, columns[2]] = grad_value.astype(jnp.bfloat16)
    for low in range(0, tokens, ATTEND_TILE):
        high = low + ATTEND_TILE
        grad_key, grad_value = block(low, high, 0, tokens, bias_ref[:, low:high])
        if low == 0:
            grad_key_ref[...] = grad_key
            grad_value_ref[...] = grad_value
        else:
            grad_key_ref[...] += grad_key
            grad_value_ref[...] += grad_value
    out_ref[:tokens, columns[1]] = grad_key_ref[...].astype(jnp.bfloat16)
    out_ref[:tokens, columns[2]] = grad_value_ref[...].astype(jnp.bfloat16)


def fixed_block(shape):
    return pl.BlockSpec(shape, lambda i: (0,) * len(shape))


def attend_specs(rows, tokens, first):
    def pair_block(part):
        return pl.BlockSpec((rows, LANES), lambda i: (0, part * PAIRS + first + i))

    specs = [pair_block(0), pair_block(1), pair_block(2)]
    masks = [fixed_block((tokens, 1)), fixed_block((1, tokens)), fixed_block((tokens, 1))]
    logs = pl.BlockSpec((1, 2, rows), lambda i: (first + i, 0, 0))
    return specs, masks, logs


def attend_forward(united_rows, masks):
    rows = united_rows.shape[0]
    tokens = masks[0].shape[0]
    specs, mask_specs, logs = attend_specs(rows, tokens, 0)
    return pl.pallas_call(
        attend_forward_kernel,
        grid=(PAIRS,),
        in_specs=specs + mask_specs,
        out_specs=[specs[0], logs],
        out_shape=[
            jax.ShapeDtypeStruct((rows, D), jnp.bfloat16),
            jax.ShapeDtypeStruct((PAIRS, 2, rows), jnp.float32),
        ],
        scratch_shapes=[pltpu.VMEM((tokens, tokens), jnp.float32)],
        name="attend_forward",
    )(united_rows, united_rows, united_rows, *masks)


def attend_backward(united_rows, grad_attended, masks, logs, first, count):
    rows = united_rows.shape[0]
    tokens = masks[0].shape[0]
    specs, mask_specs, log_spec = attend_specs(rows, tokens, first)
    width = 3 * count * LANES
    return pl.pallas_call(
        attend_backward_kernel,
        grid=(count,),
        in_specs=specs + [specs[0]] + mask_specs + [log_spec],
        out_specs=fixed_block((rows, width)),
        out_shape=jax.ShapeDtypeStruct((rows, width), jnp.bfloat16),
        scratch_shapes=[
            pltpu.VMEM((tokens, tokens), jnp.float32),
            pltpu.VMEM((tokens, LANES), jnp.float32),
            pltpu.VMEM((tokens, LANES), jnp.float32),
        ],
        name="attend_backward",
    )(united_rows, united_rows, united_rows, grad_attended, *masks, logs)


def member_rows(code_row):
    slot_ids = lax.broadcasted_iota(jnp.int32, (LANES, code_row.shape[-1]), 0)
    return (code_row == slot_ids).astype(jnp.float32).astype(jnp.bfloat16)


def split_low(values):
    high = values.astype(jnp.bfloat16)
    return high, (values - high.astype(jnp.float32)).astype(jnp.bfloat16)


def exp_similarity(query_tile, passage_rows):
    similarity = lax.dot_general(
        query_tile, passage_rows, (((1,), (1,)), ((), ())), preferred_element_type=jnp.float32
    )
    return jnp.exp(similarity * (1.0 / SOFT_TEMP))


def order_matrix(order_ref):
    count = order_ref.shape[0]
    return (order_ref[...] == lax.broadcasted_iota(jnp.int32, (count, count), 1)).astype(
        jnp.float32
    )


def own_hits(own_ref, positive_ref, rows):
    shape = (rows, positive_ref.shape[1])
    row = lax.broadcasted_iota(jnp.int32, shape, 0)
    hit = (own_ref[0] * PSG_DEV + row == positive_ref[...]) & (row < PSG_DEV)
    return row, hit.astype(jnp.float32)


def tile_forward_kernel(
    own_ref,
    query_ref,
    passage_ref,
    code_ref,
    order_ref,
    positive_ref,
    inverse_ref,
    logit_ref,
    rows_ref,
):
    step = pl.program_id(0)
    exp_sim = exp_similarity(query_ref[...], passage_ref[...])
    member = member_rows(code_ref[...])
    high, rest = split_low(exp_sim)
    bin_sums = mul_nt(high, member) + mul_nt(rest, member)
    inverse_ref[...] = 1.0 / (1.0 + bin_sums)
    terms = SOFT_TEMP * jnp.log1p(bin_sums)
    few = TILE // QLEN
    rows_ref[pl.ds(pl.multiple_of(step * few, few), few), :] = LOGIT_GAIN * jnp.sum(
        terms.reshape(-1, QLEN, LANES), axis=1
    )

    @pl.when(step == pl.num_programs(0) - 1)
    def _():
        logits = lax.dot_general(
            rows_ref[...],
            order_matrix(order_ref),
            (((0,), (0,)), ((), ())),
            precision=lax.Precision.HIGHEST,
            preferred_element_type=jnp.float32,
        )[: 2 * PSG_DEV, :]
        row, hit = own_hits(own_ref, positive_ref, 2 * PSG_DEV)
        chosen = jnp.sum(logits * hit, axis=0, keepdims=True)
        logit_ref[0] = jnp.where(row == PSG_DEV, chosen, logits)


def tile_backward_kernel(
    own_ref,
    query_ref,
    passage_ref,
    code_ref,
    order_ref,
    positive_ref,
    inverse_ref,
    own_logit_ref,
    logit_ref,
    grad_query_ref,
    grad_passage_ref,
    loss_ref,
    rows_ref,
):
    step = pl.program_id(0)

    @pl.when(step == 0)
    def _():
        grad_passage_ref[...] = jnp.zeros_like(grad_passage_ref)
        logits = logit_ref[:, :PSG_DEV, :]
        peak = jnp.max(jnp.max(logits, axis=0), axis=0, keepdims=True)
        raised = jnp.exp(logits - peak[None])
        log_norm = peak + jnp.log(jnp.sum(jnp.sum(raised, axis=0), axis=0, keepdims=True))
        loss_ref[...] = log_norm - jnp.sum(logit_ref[:, PSG_DEV, :], axis=0, keepdims=True)
        row, hit = own_hits(own_ref, positive_ref, 2 * PSG_DEV)
        grads = jnp.where(row < PSG_DEV, jnp.exp(own_logit_ref[0] - log_norm) - hit, 0.0)
        grads = jnp.concatenate(
            [grads, jnp.zeros((LANES - 2 * PSG_DEV, grads.shape[1]), jnp.float32)], axis=0
        )
        rows_ref[...] = LOGIT_GAIN * lax.dot_general(
            order_matrix(order_ref),
            grads,
            (((1,), (1,)), ((), ())),
            precision=lax.Precision.HIGHEST,
            preferred_element_type=jnp.float32,
        )

    exp_sim = exp_similarity(query_ref[...], passage_ref[...])
    member = member_rows(code_ref[...])
    few = TILE // QLEN
    grad_rows = rows_ref[pl.ds(pl.multiple_of(step * few, few), few), :]
    grad_tokens = jnp.broadcast_to(grad_rows[:, None, :], (few, QLEN, LANES)).reshape(-1, LANES)
    high, rest = split_low(grad_tokens * inverse_ref[...])
    spread = mul_nn(high, member) + mul_nn(rest, member)
    grad_sim = (exp_sim * spread).astype(jnp.bfloat16)
    grad_query_ref[...] = mul_nn(grad_sim, passage_ref[...])
    grad_passage_ref[...] += mul_tn(grad_sim, query_ref[...])


def tile_forward(own, queries, passages, codes, order, positives):
    count = queries.shape[0]
    tokens = passages.shape[0]
    rows = pl.BlockSpec((TILE, LANES), lambda i: (i, 0))
    found = order.shape[0]
    return pl.pallas_call(
        tile_forward_kernel,
        grid=(count // TILE,),
        in_specs=[
            pl.BlockSpec(memory_space=pltpu.SMEM),
            rows,
            fixed_block((tokens, PROJ)),
            fixed_block((1, tokens)),
            fixed_block((found, 1)),
            fixed_block((1, found)),
        ],
        out_specs=[rows, fixed_block((1, 2 * PSG_DEV, found))],
        out_shape=[
            jax.ShapeDtypeStruct((count, LANES), jnp.float32),
            jax.ShapeDtypeStruct((1, 2 * PSG_DEV, found), jnp.float32),
        ],
        scratch_shapes=[pltpu.VMEM((found, LANES), jnp.float32)],
        name="tile_forward",
    )(own, queries, passages, codes, order, positives)


def tile_backward(own, queries, passages, codes, order, positives, inverse, own_logits, logits):
    count = queries.shape[0]
    tokens = passages.shape[0]
    rows = pl.BlockSpec((TILE, LANES), lambda i: (i, 0))
    found = order.shape[0]
    return pl.pallas_call(
        tile_backward_kernel,
        grid=(count // TILE,),
        in_specs=[
            pl.BlockSpec(memory_space=pltpu.SMEM),
            rows,
            fixed_block((tokens, PROJ)),
            fixed_block((1, tokens)),
            fixed_block((found, 1)),
            fixed_block((1, found)),
            rows,
            fixed_block(own_logits.shape),
            fixed_block(logits.shape),
        ],
        out_specs=[rows, fixed_block((tokens, PROJ)), fixed_block((1, found))],
        out_shape=[
            jax.ShapeDtypeStruct((count, PROJ), jnp.float32),
            jax.ShapeDtypeStruct(passages.shape, jnp.float32),
            jax.ShapeDtypeStruct((1, found), jnp.float32),
        ],
        scratch_shapes=[pltpu.VMEM((found, LANES), jnp.float32)],
        name="tile_backward",
    )(own, queries, passages, codes, order, positives, inverse, own_logits, logits)


def swap_wide(part, bit):
    pairs = [(i, i ^ (1 << bit)) for i in range(lax.axis_size("pb"))]
    return lax.ppermute(part, "pb", pairs)


def swap_narrow(part, step):
    pairs = [(i, i ^ step) for i in range(lax.axis_size("pa"))]
    return lax.ppermute(part, "pa", pairs)


def wide_bits():
    count = lax.axis_size("pb").bit_length() - 1
    return list(range(1, count)) + [0]


def relative_masks():
    narrow = lax.axis_size("pa")
    masks = list(range(narrow))
    for bit in wide_bits():
        masks = masks + [m ^ (narrow << bit) for m in masks]
    return masks


def gather_relative(part):
    parts = [part] + [swap_narrow(part, s) for s in range(1, lax.axis_size("pa"))]
    whole = jnp.concatenate(parts, axis=0)
    for bit in wide_bits():
        whole = jnp.concatenate([whole, swap_wide(whole, bit)], axis=0)
    return whole


def sum_relative(whole):
    for bit in wide_bits()[::-1]:
        half = whole.shape[0] // 2
        whole = whole[:half] + swap_wide(whole[half:], bit)
    narrow = lax.axis_size("pa")
    size = whole.shape[0] // narrow
    total = whole[:size]
    for step in range(1, narrow):
        total = total + swap_narrow(whole[step * size : (step + 1) * size], step)
    return total


def chip_count():
    return lax.axis_size("pb") // 2


def write_columns(lane, values, split, full_ref, low_refs, step):
    width = values.shape[-1]

    @pl.when(step == 0)
    def _():
        full_ref[..., lane : lane + width] = values
        if split:
            full_ref[..., lane + width : lane + 2 * width] = jnp.zeros_like(values)

    for i, low_ref in enumerate(low_refs, 1):

        @pl.when(step == i)
        def _(low_ref=low_ref):
            high, rest = split_low(values)
            low_ref[..., lane : lane + width] = high
            if split:
                low_ref[..., lane + width : lane + 2 * width] = rest


def fold_kernel(place_ref, *refs, widths, received, split, sends):
    del place_ref
    own = refs[: len(widths)]
    arrived = refs[len(widths) : len(widths) + received]
    full_ref = refs[len(widths) + received]
    low_refs = refs[len(widths) + received + 1 :]
    step = pl.program_id(0)
    out_shape = full_ref.shape

    def load(ref, low, high):
        part = ref[...].reshape(out_shape[:-1] + (ref.shape[-1],))
        return part[..., low:high].astype(jnp.float32)

    lane = 0
    for ref, width in zip(own, widths):
        last = split and ref is own[-1]
        plain = width - 2 * LANES if last else width
        if plain:
            total = load(ref, 0, plain)
            for other in arrived:
                total = total + load(other, lane, lane + plain)
            write_columns(lane, total, False, full_ref, low_refs, step)
        if last:
            total = load(ref, plain, plain + LANES) + load(ref, plain + LANES, width)
            for other in arrived:
                total = total + (
                    load(other, lane + plain, lane + plain + LANES)
                    + load(other, lane + plain + LANES, lane + width)
                )
            write_columns(lane + plain, total, True, full_ref, low_refs, step)
        lane += width


class ScatterSum:
    def __init__(self, parts, split=False):
        wide = lax.axis_size("pb")
        self.narrow = lax.axis_size("pa")
        self.split = split
        self.rows = parts[0].shape[0] // (wide * self.narrow)
        self.widths = [p.shape[1] for p in parts]
        self.parts = [
            p.reshape(chip_count(), 2, self.narrow, self.rows, p.shape[1]) for p in parts
        ]
        core = lax.axis_index("pb") & 1
        send = [lax.dynamic_index_in_dim(p, 1 - core, 1, False) for p in self.parts]
        self.flight = [swap_wide(jnp.concatenate(send, axis=-1), 0)]
        self.stage = 0
        self.total = None

    def fold(self, own, own_specs, widths, arrived_spec, place, block, sends):
        fold = functools.partial(
            fold_kernel,
            widths=widths,
            received=len(self.flight),
            split=self.split,
            sends=sends,
        )
        whole = pl.BlockSpec(block, lambda i, place_ref: (0,) * len(block))
        outs = pl.pallas_call(
            fold,
            grid_spec=pltpu.PrefetchScalarGridSpec(
                num_scalar_prefetch=1,
                grid=(sends + 1,),
                in_specs=own_specs + [arrived_spec] * len(self.flight),
                out_specs=[whole] * (sends + 1),
            ),
            out_shape=[jax.ShapeDtypeStruct(block, jnp.float32)]
            + [jax.ShapeDtypeStruct(block, jnp.bfloat16)] * sends,
            name="fold_hop",
        )(place, *own, *self.flight)
        return outs[0], outs[1:]

    def advance(self):
        if self.stage == 0:
            wide_index = lax.axis_index("pb")
            place = jnp.stack([wide_index >> 1, wide_index & 1])
            chips = chip_count()
            block = (self.narrow, self.rows, sum(self.widths))

            def own_spec(width):
                return pl.BlockSpec(
                    (None, None, self.narrow, self.rows, width),
                    lambda i, place_ref: (place_ref[0] ^ i, place_ref[1], 0, 0, 0),
                )

            arrived_spec = pl.BlockSpec(
                (None,) + block, lambda i, place_ref: (place_ref[0] ^ i, 0, 0, 0)
            )
            self.kept, low = self.fold(
                self.parts,
                [own_spec(w) for w in self.widths],
                self.widths,
                arrived_spec,
                place,
                block,
                chips - 1,
            )
            pairs = lax.axis_size("pb")
            self.flight = [
                lax.ppermute(part, "pb", [(j, j ^ (i << 1)) for j in range(pairs)])
                for i, part in enumerate(low, 1)
            ]
        elif self.stage == 1:
            place = lax.axis_index("pa").reshape(1)
            columns = sum(self.widths)
            spec = pl.BlockSpec(
                (None, self.rows, columns), lambda i, place_ref: (place_ref[0] ^ i, 0, 0)
            )
            self.kept, low = self.fold(
                [self.kept], [spec], [columns], spec, place, (self.rows, columns), self.narrow - 1
            )
            self.flight = [swap_narrow(part, i) for i, part in enumerate(low, 1)]
        elif self.stage == 2:
            total = self.kept
            for part in self.flight:
                total = total + part.astype(jnp.float32)
            self.flight = []
            self.total = total
        self.stage += 1

    def finish(self):
        while self.total is None:
            self.advance()
        return self.total


def meet(chain, sums):
    flights = [s.flight for s in sums]
    chain, flights = lax.optimization_barrier((chain, flights))
    for one, flight in zip(sums, flights):
        one.flight = flight
        one.advance()
    return chain


def gelu_kernel(row_ref, weight_ref, bias_ref, active_ref, slope_ref):
    rows = row_ref.shape[0]
    part = rows // GELU_PARTS
    for low in range(0, rows, part):
        inputs = mul_nn(row_ref[low : low + part, :], weight_ref[...]) + bias_ref[...]
        ratio = 1.0 / (1.0 + TAIL_RATE * jnp.abs(inputs))
        factor = jnp.full_like(ratio, TAIL_TERMS[-1])
        for term in TAIL_TERMS[-2::-1]:
            factor = factor * ratio + term
        bell = jnp.exp(inputs * inputs * -0.5)
        tail = bell * factor
        share = jnp.where(inputs < 0.0, tail, 1.0 - tail)
        active_ref[low : low + part, :] = (inputs * share).astype(jnp.bfloat16)
        slope_ref[low : low + part, :] = (share + inputs * bell * BELL_SCALE).astype(jnp.bfloat16)


def up_gelu(rows, weight, bias):
    count, depth = rows.shape
    width = weight.shape[1]
    out = pl.BlockSpec((count, GELU_TILE), lambda i: (0, i))
    return pl.pallas_call(
        gelu_kernel,
        grid=(width // GELU_TILE,),
        in_specs=[
            fixed_block((count, depth)),
            pl.BlockSpec((depth, GELU_TILE), lambda i: (0, i)),
            pl.BlockSpec((1, GELU_TILE), lambda i: (0, i)),
        ],
        out_specs=[out, out],
        out_shape=[jax.ShapeDtypeStruct((count, width), jnp.bfloat16)] * 2,
        name="up_gelu",
    )(rows, weight, bias[None, :])


def body(
    query_states,
    passage_states,
    passage_bins,
    padding_mask,
    token_ids,
    positives,
    united_weight,
    output_weight,
    first_gain,
    first_shift,
    up_weight,
    up_bias,
    down_weight,
    second_gain,
    second_shift,
    project_weight,
):
    query_count = query_states.shape[0]
    token_count = passage_states.shape[0]
    all_rows = jnp.concatenate([passage_states, query_states], axis=0)
    united_rows = jnp.dot(all_rows, united_weight, preferred_element_type=jnp.float32).astype(
        jnp.bfloat16
    )
    bins_row = passage_bins[0]
    mask_row = padding_mask[0]
    masks = (bins_row[:, None], passage_bins, mask_row[:, None])
    attended, logs = attend_forward(united_rows, masks)
    hidden_one = all_rows.astype(jnp.float32) + jnp.dot(
        attended, output_weight, preferred_element_type=jnp.float32
    )
    norm_one = layer_norm(hidden_one, first_gain, first_shift)
    norm_one_low = norm_one.astype(jnp.bfloat16)
    active_low, slope_low = up_gelu(norm_one_low, up_weight, up_bias)
    hidden_two = norm_one + jnp.dot(active_low, down_weight, preferred_element_type=jnp.float32)
    norm_two = layer_norm(hidden_two, second_gain, second_shift)
    norm_two_low = norm_two.astype(jnp.bfloat16)
    projected = jnp.dot(norm_two_low, project_weight, preferred_element_type=jnp.float32)
    embedded = unit_rows(projected)
    embedded_low = embedded.astype(jnp.bfloat16)
    query_emb = embedded_low[token_count:]
    passage_emb = embedded_low[:token_count]
    usable = (mask_row == 1) & (token_ids[0] >= SKIP_IDS)
    own_codes = jnp.where(usable, bins_row, -1)
    own_index = lax.axis_index("pb") * lax.axis_size("pa") + lax.axis_index("pa")
    own = own_index.reshape(1)
    queries_here = query_count // QLEN
    blocks = own_index ^ jnp.array(relative_masks(), jnp.int32)
    order = (
        blocks[:, None] * queries_here + lax.broadcasted_iota(jnp.int32, (1, queries_here), 1)
    ).reshape(-1, 1)
    all_queries = gather_relative(query_emb)
    code_row = own_codes[None, :]
    wanted = positives[None, :]
    inverse, own_logits = tile_forward(own, all_queries, passage_emb, code_row, order, wanted)
    logits = gather_relative(own_logits)
    all_grad, grad_passage_emb, losses = tile_backward(
        own, all_queries, passage_emb, code_row, order, wanted, inverse, own_logits, logits
    )
    own_losses = lax.dynamic_slice_in_dim(losses[0], own_index * queries_here, queries_here)
    grad_query_emb = sum_relative(all_grad)
    grad_embedded = jnp.concatenate([grad_passage_emb, grad_query_emb], axis=0)
    unit_pull = jax.vjp(unit_rows, projected)[1]
    grad_projected = unit_pull(grad_embedded)[0].astype(jnp.bfloat16)
    grad_project = contract_rows(norm_two_low, grad_projected)
    grad_norm_two = times_transposed(grad_projected, project_weight)
    second_pull = jax.vjp(layer_norm, hidden_two, second_gain, second_shift)[1]
    grad_hidden_two, grad_second_gain, grad_second_shift = second_pull(grad_norm_two)
    grad_branch_two = grad_hidden_two.astype(jnp.bfloat16)
    down_sum = ScatterSum([contract_rows(active_low, grad_branch_two)])
    grad_active = times_transposed(grad_branch_two, down_weight)
    grad_up_rows = (grad_active * slope_low.astype(jnp.float32)).astype(jnp.bfloat16)
    grad_up_rows = meet(grad_up_rows, [down_sum])
    grad_up_bias = jnp.sum(grad_up_rows, axis=0, dtype=jnp.float32)
    up_sum = ScatterSum([contract_rows(norm_one_low, grad_up_rows)])
    grad_norm_one = times_transposed(grad_up_rows, up_weight) + grad_hidden_two
    first_pull = jax.vjp(layer_norm, hidden_one, first_gain, first_shift)[1]
    grad_hidden_one, grad_first_gain, grad_first_shift = first_pull(grad_norm_one)
    grad_branch_one = grad_hidden_one.astype(jnp.bfloat16)
    grad_branch_one = meet(grad_branch_one, [up_sum])
    grad_output = contract_rows(attended, grad_branch_one)
    devices = lax.axis_size("pb") * lax.axis_size("pa")
    vectors = jnp.concatenate(
        [
            v.reshape(devices, D // devices, -1)
            for v in (
                grad_first_gain, grad_first_shift, grad_second_gain, grad_second_shift, grad_up_bias
            )
        ],
        axis=-1,
    ).reshape(D, -1)
    vectors = jnp.pad(vectors, ((0, 0), (0, LANES - vectors.shape[1])))
    extra = jnp.concatenate((grad_project,) + split_low(vectors), axis=1)
    grad_attended = times_transposed(grad_branch_one, output_weight).astype(jnp.bfloat16)
    grad_united_rows = attend_backward(united_rows, grad_attended, masks, logs, 0, PAIRS)
    grad_united_rows = meet(grad_united_rows, [down_sum, up_sum])
    late_sum = ScatterSum([contract_rows(all_rows, grad_united_rows), grad_output, extra], True)
    grad_rows = times_transposed(grad_united_rows, united_weight) + grad_hidden_one
    late = late_sum.finish()
    down_total = down_sum.finish()
    up_total = up_sum.finish()
    united_total, output_total, project_total, small, rest = jnp.split(
        late, [3 * D, 4 * D, 4 * D + PROJ, 4 * D + PROJ + LANES], axis=1
    )
    small = small + rest
    shared = (
        united_total,
        output_total,
        small[:, 0],
        small[:, 1],
        up_total,
        small[:, 4:8].reshape(-1),
        down_total,
        small[:, 2],
        small[:, 3],
        project_total,
    )
    return (
        query_emb,
        passage_emb,
        own_losses,
        grad_rows[token_count:],
        grad_rows[:token_count],
        shared[0],
        shared[1],
        shared[2],
        shared[3],
        shared[4],
        shared[5],
        shared[6],
        shared[7],
        shared[8],
        shared[9],
    )


def solution(mesh):
    return jax.shard_map(
        body,
        mesh=mesh,
        in_specs=(
            P(("pb", "pa"), None),
            P(("pb", "pa"), None),
            P(("pb", "pa"), None),
            P(("pb", "pa"), None),
            P(("pb", "pa"), None),
            P(),
            P(),
            P(),
            P(),
            P(),
            P(),
            P(),
            P(),
            P(),
            P(),
            P(),
        ),
        out_specs=(
            P(("pb", "pa"), None),
            P(("pb", "pa"), None),
            P(("pb", "pa")),
            P(("pb", "pa"), None),
            P(("pb", "pa"), None),
            P(("pb", "pa"), None),
            P(("pb", "pa"), None),
            P(("pb", "pa")),
            P(("pb", "pa")),
            P(("pb", "pa"), None),
            P(("pb", "pa")),
            P(("pb", "pa"), None),
            P(("pb", "pa")),
            P(("pb", "pa")),
            P(("pb", "pa"), None),
        ),
        check_vma=False,
    )
```

```python
import functools

import jax
import jax.numpy as jnp
from jax import lax
from jax.experimental import pallas as pl
from jax.experimental.pallas import tpu as pltpu
from jax.sharding import PartitionSpec as P

D = 768
HEAD_DIM = 64
HEADS = 12
PROJ = 128
QLEN = 32
PSG_DEV = 4
SKIP_IDS = 3000
LANES = 128
TILE = 256
ATTEND_TILE = 256
PAIRS = D // LANES
FF_TILE = 512
ROW_PARTS = 2
VECTOR_LANES = 256
TAIL_RATE = 0.23
TAIL_TERMS = (
    -2.7766233e-05,
    0.09237861,
    0.08576121,
    0.119523115,
    -0.03294691,
    0.3015191,
    -0.27817392,
    0.29043987,
    -0.07847336,
)
BELL_SCALE = 0.3989422804014327


SOFT_TEMP = 0.1
LOGIT_GAIN = 8.0
NORM_EPSILON = 1e-06
MASK_FILL = -1000000000.0
SCORE_SCALE = 0.125


def contract_rows(operand, partner):
    summed = jnp.einsum("rd,re->de", operand, partner, preferred_element_type=jnp.float32)
    return summed.astype(jnp.bfloat16)


def times_transposed(operand, partner):
    return jnp.einsum("re,de->rd", operand, partner, preferred_element_type=jnp.float32)


def head_part(values, head):
    lane = lax.broadcasted_iota(jnp.int32, values.shape, 1)
    return jnp.where(lane // HEAD_DIM == head, values, jnp.zeros_like(values))


def mul_nt(operand, partner):
    return lax.dot_general(
        operand, partner, (((1,), (1,)), ((), ())), preferred_element_type=jnp.float32
    )


def mul_tn(operand, partner):
    return lax.dot_general(
        operand, partner, (((0,), (0,)), ((), ())), preferred_element_type=jnp.float32
    )


def mul_nn(operand, partner):
    return jnp.dot(operand, partner, preferred_element_type=jnp.float32)


def write_bias(bias_ref, bin_column_ref, bin_row_ref, mask_column_ref):
    @pl.when(pl.program_id(0) == 0)
    def _():
        keys = lax.broadcasted_iota(jnp.int32, bias_ref.shape, 0)
        queries = lax.broadcasted_iota(jnp.int32, bias_ref.shape, 1)
        allowed = (bin_column_ref[...] == bin_row_ref[...]) & (
            (mask_column_ref[...] == 1) | (keys == queries)
        )
        bias_ref[...] = jnp.where(allowed, 0.0, MASK_FILL)


def query_bias(count):
    keys = lax.broadcasted_iota(jnp.int32, (count, count), 0) // QLEN
    queries = lax.broadcasted_iota(jnp.int32, (count, count), 1) // QLEN
    return jnp.where(keys == queries, 0.0, MASK_FILL)


def attend_forward_kernel(
    q_ref, k_ref, v_ref, bin_column_ref, bin_row_ref, mask_column_ref, out_ref, log_ref, bias_ref
):
    write_bias(bias_ref, bin_column_ref, bin_row_ref, mask_column_ref)
    tokens = bias_ref.shape[0]
    rows = q_ref.shape[0]

    def block(low, high, key_low, key_high, bias):
        query = q_ref[low:high, :] * SCORE_SCALE
        key = k_ref[key_low:key_high, :]
        value = v_ref[key_low:key_high, :]
        out = None
        for head in range(2):
            scores = mul_nt(head_part(key, head), query) + bias
            peak = jnp.max(scores, axis=0, keepdims=True)
            raised = jnp.exp(scores - peak)
            total = jnp.sum(raised, axis=0, keepdims=True)
            log_ref[0, head : head + 1, low:high] = peak + jnp.log(total)
            weights = (raised * (1.0 / total)).astype(jnp.bfloat16)
            part = mul_tn(weights, head_part(value, head))
            out = part if out is None else out + part
        out_ref[low:high, :] = out.astype(jnp.bfloat16)

    block(tokens, rows, tokens, rows, query_bias(rows - tokens))
    for low in range(0, tokens, ATTEND_TILE):
        high = low + ATTEND_TILE
        block(low, high, 0, tokens, bias_ref[:, low:high])


def attend_backward_kernel(
    q_ref,
    k_ref,
    v_ref,
    grad_ref,
    bin_column_ref,
    bin_row_ref,
    mask_column_ref,
    log_ref,
    out_ref,
    bias_ref,
    grad_key_ref,
    grad_value_ref,
):
    write_bias(bias_ref, bin_column_ref, bin_row_ref, mask_column_ref)
    tokens = bias_ref.shape[0]
    rows = q_ref.shape[0]
    width = out_ref.shape[1] // 3
    base = pl.program_id(0) * LANES
    columns = [pl.ds(pl.multiple_of(base + i * width, LANES), LANES) for i in range(3)]

    def block(low, high, key_low, key_high, bias):
        query = q_ref[low:high, :] * SCORE_SCALE
        grad = grad_ref[low:high, :]
        key = k_ref[key_low:key_high, :]
        value = v_ref[key_low:key_high, :]
        sums = None
        for head in range(2):
            own_key = head_part(key, head)
            scores = mul_nt(own_key, query) + bias
            weights = jnp.exp(scores - log_ref[0, head : head + 1, low:high])
            weighted = weights * mul_nt(head_part(value, head), grad)
            centre = jnp.sum(weighted, axis=0, keepdims=True)
            grad_scores = (weighted - weights * centre).astype(jnp.bfloat16)
            parts = (
                mul_tn(grad_scores, own_key),
                mul_nn(grad_scores, head_part(query, head)),
                mul_nn(weights.astype(jnp.bfloat16), head_part(grad, head)),
            )
            sums = parts if sums is None else tuple(a + b for a, b in zip(sums, parts))
        out_ref[low:high, columns[0]] = (sums[0] * SCORE_SCALE).astype(jnp.bfloat16)
        return sums[1:]

    grad_key, grad_value = block(tokens, rows, tokens, rows, query_bias(rows - tokens))
    out_ref[tokens:, columns[1]] = grad_key.astype(jnp.bfloat16)
    out_ref[tokens:, columns[2]] = grad_value.astype(jnp.bfloat16)
    for low in range(0, tokens, ATTEND_TILE):
        high = low + ATTEND_TILE
        grad_key, grad_value = block(low, high, 0, tokens, bias_ref[:, low:high])
        if low == 0:
            grad_key_ref[...] = grad_key
            grad_value_ref[...] = grad_value
        else:
            grad_key_ref[...] += grad_key
            grad_value_ref[...] += grad_value
    out_ref[:tokens, columns[1]] = grad_key_ref[...].astype(jnp.bfloat16)
    out_ref[:tokens, columns[2]] = grad_value_ref[...].astype(jnp.bfloat16)


def fixed_block(shape):
    return pl.BlockSpec(shape, lambda i: (0,) * len(shape))


def attend_specs(rows, tokens, first):
    def pair_block(part):
        return pl.BlockSpec((rows, LANES), lambda i: (0, part * PAIRS + first + i))

    specs = [pair_block(0), pair_block(1), pair_block(2)]
    masks = [fixed_block((tokens, 1)), fixed_block((1, tokens)), fixed_block((tokens, 1))]
    logs = pl.BlockSpec((1, 2, rows), lambda i: (first + i, 0, 0))
    return specs, masks, logs


def attend_forward(united_rows, masks):
    rows = united_rows.shape[0]
    tokens = masks[0].shape[0]
    specs, mask_specs, logs = attend_specs(rows, tokens, 0)
    return pl.pallas_call(
        attend_forward_kernel,
        grid=(PAIRS,),
        in_specs=specs + mask_specs,
        out_specs=[specs[0], logs],
        out_shape=[
            jax.ShapeDtypeStruct((rows, D), jnp.bfloat16),
            jax.ShapeDtypeStruct((PAIRS, 2, rows), jnp.float32),
        ],
        scratch_shapes=[pltpu.VMEM((tokens, tokens), jnp.float32)],
        name="attend_forward",
    )(united_rows, united_rows, united_rows, *masks)


def attend_backward(united_rows, grad_attended, masks, logs, first, count):
    rows = united_rows.shape[0]
    tokens = masks[0].shape[0]
    specs, mask_specs, log_spec = attend_specs(rows, tokens, first)
    width = 3 * count * LANES
    return pl.pallas_call(
        attend_backward_kernel,
        grid=(count,),
        in_specs=specs + [specs[0]] + mask_specs + [log_spec],
        out_specs=fixed_block((rows, width)),
        out_shape=jax.ShapeDtypeStruct((rows, width), jnp.bfloat16),
        scratch_shapes=[
            pltpu.VMEM((tokens, tokens), jnp.float32),
            pltpu.VMEM((tokens, LANES), jnp.float32),
            pltpu.VMEM((tokens, LANES), jnp.float32),
        ],
        name="attend_backward",
    )(united_rows, united_rows, united_rows, grad_attended, *masks, logs)


def member_rows(code_row):
    slot_ids = lax.broadcasted_iota(jnp.int32, (LANES, code_row.shape[-1]), 0)
    return (code_row == slot_ids).astype(jnp.float32).astype(jnp.bfloat16)


def split_low(values):
    high = values.astype(jnp.bfloat16)
    return high, (values - high.astype(jnp.float32)).astype(jnp.bfloat16)


def exp_similarity(query_tile, passage_rows):
    similarity = lax.dot_general(
        query_tile, passage_rows, (((1,), (1,)), ((), ())), preferred_element_type=jnp.float32
    )
    return jnp.exp(similarity * (1.0 / SOFT_TEMP))


def order_matrix(order_ref):
    count = order_ref.shape[0]
    return (order_ref[...] == lax.broadcasted_iota(jnp.int32, (count, count), 1)).astype(
        jnp.float32
    )


def own_hits(own_ref, positive_ref, rows):
    shape = (rows, positive_ref.shape[1])
    row = lax.broadcasted_iota(jnp.int32, shape, 0)
    hit = (own_ref[0] * PSG_DEV + row == positive_ref[...]) & (row < PSG_DEV)
    return row, hit.astype(jnp.float32)


def tile_forward_kernel(
    own_ref,
    near_ref,
    far_ref,
    passage_ref,
    code_ref,
    order_ref,
    positive_ref,
    inverse_ref,
    logit_ref,
    rows_ref,
):
    step = pl.program_id(0)
    query = jnp.where(step < pl.num_programs(0) // 2, near_ref[...], far_ref[...])
    exp_sim = exp_similarity(query, passage_ref[...])
    member = member_rows(code_ref[...])
    high, rest = split_low(exp_sim)
    bin_sums = mul_nt(high, member) + mul_nt(rest, member)
    inverse_ref[...] = 1.0 / (1.0 + bin_sums)
    terms = SOFT_TEMP * jnp.log1p(bin_sums)
    few = TILE // QLEN
    rows_ref[pl.ds(pl.multiple_of(step * few, few), few), :] = LOGIT_GAIN * jnp.sum(
        terms.reshape(-1, QLEN, LANES), axis=1
    )

    @pl.when(step == pl.num_programs(0) - 1)
    def _():
        logits = lax.dot_general(
            rows_ref[...],
            order_matrix(order_ref),
            (((0,), (0,)), ((), ())),
            precision=lax.Precision.HIGHEST,
            preferred_element_type=jnp.float32,
        )[: 2 * PSG_DEV, :]
        row, hit = own_hits(own_ref, positive_ref, 2 * PSG_DEV)
        chosen = jnp.sum(logits * hit, axis=0, keepdims=True)
        logit_ref[0] = jnp.where(row == PSG_DEV, chosen, logits)


def tile_backward_kernel(
    own_ref,
    near_ref,
    far_ref,
    passage_ref,
    code_ref,
    order_ref,
    positive_ref,
    inverse_ref,
    own_logit_ref,
    near_logit_ref,
    far_logit_ref,
    grad_near_ref,
    grad_far_ref,
    grad_passage_ref,
    loss_ref,
    rows_ref,
):
    step = pl.program_id(0)

    @pl.when(step == 0)
    def _():
        grad_passage_ref[...] = jnp.zeros_like(grad_passage_ref)
        halves = (near_logit_ref, far_logit_ref)
        peaks = [
            jnp.max(jnp.max(h[:, :PSG_DEV, :], axis=0), axis=0, keepdims=True) for h in halves
        ]
        peak = jnp.maximum(peaks[0], peaks[1])
        summed = [
            jnp.sum(
                jnp.sum(jnp.exp(h[:, :PSG_DEV, :] - peak[None]), axis=0), axis=0, keepdims=True
            )
            for h in halves
        ]
        log_norm = peak + jnp.log(summed[0] + summed[1])
        chosen = [jnp.sum(h[:, PSG_DEV, :], axis=0, keepdims=True) for h in halves]
        loss_ref[...] = log_norm - (chosen[0] + chosen[1])
        row, hit = own_hits(own_ref, positive_ref, 2 * PSG_DEV)
        grads = jnp.where(row < PSG_DEV, jnp.exp(own_logit_ref[0] - log_norm) - hit, 0.0)
        grads = jnp.concatenate(
            [grads, jnp.zeros((LANES - 2 * PSG_DEV, grads.shape[1]), jnp.float32)], axis=0
        )
        rows_ref[...] = LOGIT_GAIN * lax.dot_general(
            order_matrix(order_ref),
            grads,
            (((1,), (1,)), ((), ())),
            precision=lax.Precision.HIGHEST,
            preferred_element_type=jnp.float32,
        )

    near = step < pl.num_programs(0) // 2
    query = jnp.where(near, near_ref[...], far_ref[...])
    exp_sim = exp_similarity(query, passage_ref[...])
    member = member_rows(code_ref[...])
    few = TILE // QLEN
    grad_rows = rows_ref[pl.ds(pl.multiple_of(step * few, few), few), :]
    grad_tokens = jnp.broadcast_to(grad_rows[:, None, :], (few, QLEN, LANES)).reshape(-1, LANES)
    high, rest = split_low(grad_tokens * inverse_ref[...])
    spread = mul_nn(high, member) + mul_nn(rest, member)
    grad_sim = (exp_sim * spread).astype(jnp.bfloat16)
    grad_query = mul_nn(grad_sim, passage_ref[...])

    @pl.when(near)
    def _():
        grad_near_ref[...] = grad_query

    @pl.when(jnp.logical_not(near))
    def _():
        grad_far_ref[...] = grad_query

    grad_passage_ref[...] += mul_tn(grad_sim, query)


def half_specs(count):
    half = count // TILE // 2
    return (
        pl.BlockSpec((TILE, LANES), lambda i: (jnp.minimum(i, half - 1), 0)),
        pl.BlockSpec((TILE, LANES), lambda i: (jnp.maximum(i - half, 0), 0)),
    )


def tile_forward(own, near, far, passages, codes, order, positives):
    count = 2 * near.shape[0]
    tokens = passages.shape[0]
    found = order.shape[0]
    return pl.pallas_call(
        tile_forward_kernel,
        grid=(count // TILE,),
        in_specs=[
            pl.BlockSpec(memory_space=pltpu.SMEM),
            *half_specs(count),
            fixed_block((tokens, PROJ)),
            fixed_block((1, tokens)),
            fixed_block((found, 1)),
            fixed_block((1, found)),
        ],
        out_specs=[
            pl.BlockSpec((TILE, LANES), lambda i: (i, 0)),
            fixed_block((1, 2 * PSG_DEV, found)),
        ],
        out_shape=[
            jax.ShapeDtypeStruct((count, LANES), jnp.float32),
            jax.ShapeDtypeStruct((1, 2 * PSG_DEV, found), jnp.float32),
        ],
        scratch_shapes=[pltpu.VMEM((found, LANES), jnp.float32)],
        name="tile_forward",
    )(own, near, far, passages, codes, order, positives)


def tile_backward(
    own, near, far, passages, codes, order, positives, inverse, own_logits, near_logits, far_logits
):
    count = 2 * near.shape[0]
    tokens = passages.shape[0]
    found = order.shape[0]
    halves = half_specs(count)
    return pl.pallas_call(
        tile_backward_kernel,
        grid=(count // TILE,),
        in_specs=[
            pl.BlockSpec(memory_space=pltpu.SMEM),
            *halves,
            fixed_block((tokens, PROJ)),
            fixed_block((1, tokens)),
            fixed_block((found, 1)),
            fixed_block((1, found)),
            pl.BlockSpec((TILE, LANES), lambda i: (i, 0)),
            fixed_block(own_logits.shape),
            fixed_block(near_logits.shape),
            fixed_block(far_logits.shape),
        ],
        out_specs=[*halves, fixed_block((tokens, PROJ)), fixed_block((1, found))],
        out_shape=[
            jax.ShapeDtypeStruct((count // 2, PROJ), jnp.float32),
            jax.ShapeDtypeStruct((count // 2, PROJ), jnp.float32),
            jax.ShapeDtypeStruct(passages.shape, jnp.float32),
            jax.ShapeDtypeStruct((1, found), jnp.float32),
        ],
        scratch_shapes=[pltpu.VMEM((found, LANES), jnp.float32)],
        name="tile_backward",
    )(
        own,
        near,
        far,
        passages,
        codes,
        order,
        positives,
        inverse,
        own_logits,
        near_logits,
        far_logits,
    )


def swap_wide(part, bit):
    pairs = [(i, i ^ (1 << bit)) for i in range(lax.axis_size("pb"))]
    return lax.ppermute(part, "pb", pairs)


def swap_narrow(part, step):
    pairs = [(i, i ^ step) for i in range(lax.axis_size("pa"))]
    return lax.ppermute(part, "pa", pairs)


def swap_chip(part, step):
    pairs = [(i, i ^ (step << 1)) for i in range(lax.axis_size("pb"))]
    return lax.ppermute(part, "pb", pairs)


def relative_masks():
    narrow = lax.axis_size("pa")
    return [
        ((chip << 1) | core) * narrow + place
        for core in range(2)
        for chip in range(chip_count())
        for place in range(narrow)
    ]


def gather_relative(part):
    parts = [part] + [swap_narrow(part, s) for s in range(1, lax.axis_size("pa"))]
    near = jnp.concatenate(parts, axis=0)
    parts = [near] + [swap_chip(near, s) for s in range(1, chip_count())]
    near = jnp.concatenate(parts, axis=0)
    return near, swap_wide(near, 0)


def sum_relative(near, far):
    whole = near + swap_wide(far, 0)
    for count, swap in ((chip_count(), swap_chip), (lax.axis_size("pa"), swap_narrow)):
        size = whole.shape[0] // count
        total = whole[:size]
        for step in range(1, count):
            total = total + swap(whole[step * size : (step + 1) * size], step)
        whole = total
    return whole


def chip_count():
    return lax.axis_size("pb") // 2


def fold_kernel(place_ref, *refs, widths, received, split):
    del place_ref
    own = refs[: len(widths)]
    arrived = refs[len(widths) : len(widths) + received]
    outs = refs[len(widths) + received :]
    step = pl.program_id(0)
    planes = outs[0].shape[0] if len(outs[0].shape) == 3 else None

    def pick(ref, plane, low, high):
        part = ref[:, low:high] if planes is None else ref[plane, :, low:high]
        return part.astype(jnp.float32)

    def fold(plane, out_ref, full):
        lane = 0
        for ref, width in zip(own, widths):
            cut = width - VECTOR_LANES if split and ref is own[-1] else width
            for low, high in ((0, cut), (cut, width)):
                if low < high:
                    store(ref, plane, out_ref, full, lane, low, high, low > 0 or cut == 0)
            lane += width

    def store(ref, plane, out_ref, full, lane, low, high, packed):
        total = pick(ref, plane, low, high)
        for other in arrived:
            total = total + pick(other, plane, lane + low, lane + high)
        if packed:
            value = total[0:1] + total[1:2]
            first, second = (value, jnp.zeros_like(value)) if full else split_low(value)
            row = lax.broadcasted_iota(jnp.int32, total.shape, 0)
            second = jnp.where(row == 1, second.astype(jnp.float32), 0.0)
            total = jnp.where(row == 0, first.astype(jnp.float32), second)
        total = total.astype(out_ref.dtype)
        if planes is None:
            out_ref[:, lane + low : lane + high] = total
        else:
            out_ref[plane, :, lane + low : lane + high] = total

    for i, out_ref in enumerate(outs):

        @pl.when(step == i)
        def _(i=i, out_ref=out_ref):
            if planes is None:
                fold(0, out_ref, i == 0)
            else:

                @pl.loop(0, planes)
                def _(plane):
                    fold(plane, out_ref, i == 0)


def pick_kernel(core_ref, *refs):
    del core_ref
    out_ref = refs[-1]
    lane = 0
    for ref in refs[:-1]:
        width = ref.shape[-1]
        out_ref[:, :, lane : lane + width] = ref[...]
        lane += width


class ScatterSum:
    def __init__(self, parts, split=False):
        wide = lax.axis_size("pb")
        self.narrow = lax.axis_size("pa")
        self.split = split
        self.rows = parts[0].shape[0] // (wide * self.narrow)
        self.widths = [p.shape[1] for p in parts]
        self.parts = [
            p.reshape(chip_count(), 2, self.narrow, self.rows, p.shape[1]) for p in parts
        ]
        self.stage = -1
        self.total = None
        self.kept = None
        self.flight = []
        self.ready = [self.picked()]

    def picked(self):
        chips = chip_count()
        core = (lax.axis_index("pb") & 1).reshape(1)
        columns = sum(self.widths)
        return pl.pallas_call(
            pick_kernel,
            grid_spec=pltpu.PrefetchScalarGridSpec(
                num_scalar_prefetch=1,
                grid=(chips,),
                in_specs=[
                    pl.BlockSpec(
                        (None, None, self.narrow, self.rows, w),
                        lambda i, core_ref: (i, 1 - core_ref[0], 0, 0, 0),
                    )
                    for w in self.widths
                ],
                out_specs=pl.BlockSpec(
                    (None, self.narrow, self.rows, columns), lambda i, core_ref: (i, 0, 0, 0)
                ),
            ),
            out_shape=jax.ShapeDtypeStruct(
                (chips, self.narrow, self.rows, columns), jnp.bfloat16
            ),
            name="pick_half",
        )(core, *self.parts)

    def fold(self, own, own_specs, widths, arrived_spec, place, block, sends):
        fold = functools.partial(
            fold_kernel, widths=widths, received=len(self.flight), split=self.split
        )
        whole = pl.BlockSpec(block, lambda i, place_ref: (0,) * len(block))
        outs = pl.pallas_call(
            fold,
            grid_spec=pltpu.PrefetchScalarGridSpec(
                num_scalar_prefetch=1,
                grid=(sends + 1,),
                in_specs=own_specs + [arrived_spec] * len(self.flight),
                out_specs=[whole] * (sends + 1),
            ),
            out_shape=[jax.ShapeDtypeStruct(block, jnp.float32)]
            + [jax.ShapeDtypeStruct(block, jnp.bfloat16)] * sends,
            name="fold_hop",
        )(place, *own, *self.flight)
        self.kept, self.ready = outs[0], outs[1:]

    def fold_wide(self):
        wide_index = lax.axis_index("pb")
        place = jnp.stack([wide_index >> 1, wide_index & 1])
        block = (self.narrow, self.rows, sum(self.widths))

        def own_spec(width):
            return pl.BlockSpec(
                (None, None, self.narrow, self.rows, width),
                lambda i, place_ref: (place_ref[0] ^ i, place_ref[1], 0, 0, 0),
            )

        arrived_spec = pl.BlockSpec(
            (None,) + block, lambda i, place_ref: (place_ref[0] ^ i, 0, 0, 0)
        )
        specs = [own_spec(w) for w in self.widths]
        self.fold(self.parts, specs, self.widths, arrived_spec, place, block, chip_count() - 1)

    def fold_narrow(self):
        place = lax.axis_index("pa").reshape(1)
        columns = sum(self.widths)
        spec = pl.BlockSpec(
            (None, self.rows, columns), lambda i, place_ref: (place_ref[0] ^ i, 0, 0)
        )
        self.fold([self.kept], [spec], [columns], spec, place, spec.block_shape[1:], self.narrow - 1)

    def take(self):
        if self.stage == 0:
            self.fold_wide()
        elif self.stage == 1:
            self.fold_narrow()
        else:
            total = self.kept
            for part in self.flight:
                total = total + part.astype(jnp.float32)
            self.total = total
            self.ready = []

    def send(self):
        self.stage += 1
        if self.stage == 0:
            self.flight = [swap_wide(self.ready[0], 0)]
            return
        swap = swap_chip if self.stage == 1 else swap_narrow
        self.flight = [swap(part, i) for i, part in enumerate(self.ready, 1)]

    def finish(self):
        if self.stage < 0:
            self.send()
        while self.total is None:
            self.take()
            self.send()
        return self.total


def start(chain, sums):
    chain, ready = lax.optimization_barrier((chain, [s.ready for s in sums]))
    for one, blocks in zip(sums, ready):
        one.ready = blocks
        one.send()
    return chain


def meet(chain, sums):
    chain, flights = lax.optimization_barrier((chain, [s.flight for s in sums]))
    for one, flight in zip(sums, flights):
        one.flight = flight
        one.take()
    return start(chain, sums)


def row_loop(rows):
    size = rows // ROW_PARTS

    def wrap(work):
        @pl.loop(0, ROW_PARTS)
        def _(i):
            work(pl.ds(pl.multiple_of(i * size, size), size))

    return wrap


def normed(hidden):
    centred = hidden - jnp.mean(hidden, axis=-1, keepdims=True)
    spread = jnp.mean(centred * centred, axis=-1, keepdims=True)
    scale = lax.rsqrt(spread + NORM_EPSILON)
    return centred * scale, scale


def encode_kernel(
    row_ref,
    attended_ref,
    output_weight_ref,
    first_gain_ref,
    first_shift_ref,
    up_weight_ref,
    up_bias_ref,
    down_weight_ref,
    second_gain_ref,
    second_shift_ref,
    project_ref,
    unit_one_ref,
    scale_one_ref,
    low_one_ref,
    active_ref,
    slope_ref,
    unit_two_ref,
    scale_two_ref,
    low_two_ref,
    projected_ref,
    passage_ref,
    query_ref,
    sum_ref,
    embedded_ref,
):
    step = pl.program_id(0)
    rows = row_ref.shape[0]
    tokens = passage_ref.shape[0]

    @pl.when(step == 0)
    def _():
        @row_loop(rows)
        def _(part):
            hidden = row_ref[part, :].astype(jnp.float32) + mul_nn(
                attended_ref[part, :], output_weight_ref[...]
            )
            unit, scale = normed(hidden)
            norm_one = unit * first_gain_ref[...] + first_shift_ref[...]
            unit_one_ref[part, :] = unit
            scale_one_ref[part, :] = scale
            low_one_ref[part, :] = norm_one.astype(jnp.bfloat16)
            sum_ref[part, :] = norm_one

    part = rows // ROW_PARTS
    for low in range(0, rows, part):
        inputs = mul_nn(low_one_ref[low : low + part, :], up_weight_ref[...]) + up_bias_ref[...]
        ratio = 1.0 / (1.0 + TAIL_RATE * jnp.abs(inputs))
        factor = jnp.full_like(ratio, TAIL_TERMS[-1])
        for term in TAIL_TERMS[-2::-1]:
            factor = factor * ratio + term
        bell = jnp.exp(inputs * inputs * -0.5)
        tail = bell * factor
        share = jnp.where(inputs < 0.0, tail, 1.0 - tail)
        active = (inputs * share).astype(jnp.bfloat16)
        active_ref[low : low + part, :] = active
        slope_ref[low : low + part, :] = (share + inputs * bell * BELL_SCALE).astype(jnp.bfloat16)
        sum_ref[low : low + part, :] += mul_nn(active, down_weight_ref[...])

    @pl.when(step == pl.num_programs(0) - 1)
    def _():
        @row_loop(rows)
        def _(part):
            unit, scale = normed(sum_ref[part, :])
            unit_two_ref[part, :] = unit
            scale_two_ref[part, :] = scale
            low_two = (unit * second_gain_ref[...] + second_shift_ref[...]).astype(jnp.bfloat16)
            low_two_ref[part, :] = low_two
            projected = mul_nn(low_two, project_ref[...])
            projected_ref[part, :] = projected
            embedded_ref[part, :] = unit_rows(projected)[0].astype(jnp.bfloat16)

        passage_ref[...] = embedded_ref[:tokens, :]
        query_ref[...] = embedded_ref[tokens:, :]


def unit_rows(projected):
    scale = lax.rsqrt(jnp.sum(projected * projected, axis=-1, keepdims=True) + NORM_EPSILON)
    return projected * scale, scale


def encode(
    rows_in,
    attended,
    tokens,
    output_weight,
    first_gain,
    first_shift,
    up_weight,
    up_bias,
    down_weight,
    second_gain,
    second_shift,
    project_weight,
):
    rows = rows_in.shape[0]
    width = up_weight.shape[1]
    full = fixed_block((rows, D))
    vector = fixed_block((1, D))
    column = fixed_block((rows, 1))
    chunk = pl.BlockSpec((rows, FF_TILE), lambda i: (0, i))
    low_type, full_type = jnp.bfloat16, jnp.float32
    outs = [
        (full, (rows, D), full_type),
        (column, (rows, 1), full_type),
        (full, (rows, D), low_type),
        (chunk, (rows, width), low_type),
        (chunk, (rows, width), low_type),
        (full, (rows, D), full_type),
        (column, (rows, 1), full_type),
        (full, (rows, D), low_type),
        (fixed_block((rows, PROJ)), (rows, PROJ), full_type),
        (fixed_block((tokens, PROJ)), (tokens, PROJ), low_type),
        (fixed_block((rows - tokens, PROJ)), (rows - tokens, PROJ), low_type),
    ]
    return pl.pallas_call(
        encode_kernel,
        grid=(width // FF_TILE,),
        in_specs=[
            full,
            full,
            fixed_block((D, D)),
            vector,
            vector,
            pl.BlockSpec((D, FF_TILE), lambda i: (0, i)),
            pl.BlockSpec((1, FF_TILE), lambda i: (0, i)),
            pl.BlockSpec((FF_TILE, D), lambda i: (i, 0)),
            vector,
            vector,
            fixed_block((D, PROJ)),
        ],
        out_specs=[spec for spec, _, _ in outs],
        out_shape=[jax.ShapeDtypeStruct(shape, kind) for _, shape, kind in outs],
        scratch_shapes=[
            pltpu.VMEM((rows, D), jnp.float32),
            pltpu.VMEM((rows, PROJ), jnp.bfloat16),
        ],
        name="encode",
    )(
        rows_in,
        attended,
        output_weight,
        first_gain[None],
        first_shift[None],
        up_weight,
        up_bias[None],
        down_weight,
        second_gain[None],
        second_shift[None],
        project_weight,
    )


def norm_backward(grad, unit, scale, gain):
    pulled = grad * gain
    mean = jnp.mean(pulled, axis=-1, keepdims=True)
    along = jnp.mean(pulled * unit, axis=-1, keepdims=True)
    return scale * (pulled - mean - unit * along)


def down_backward_kernel(
    grad_passage_ref,
    grad_query_ref,
    projected_ref,
    low_two_ref,
    unit_two_ref,
    scale_two_ref,
    gain_ref,
    project_ref,
    active_ref,
    slope_ref,
    down_weight_ref,
    grad_project_ref,
    grad_hidden_ref,
    grad_gain_ref,
    grad_shift_ref,
    grad_down_ref,
    grad_up_rows_ref,
    grad_bias_ref,
    grad_low_ref,
    branch_ref,
    grad_rows_ref,
):
    rows = projected_ref.shape[0]
    tokens = grad_passage_ref.shape[0]

    @pl.when(pl.program_id(0) == 0)
    def _():
        grad_gain_ref[...] = jnp.zeros_like(grad_gain_ref)
        grad_shift_ref[...] = jnp.zeros_like(grad_shift_ref)
        grad_rows_ref[:tokens, :] = grad_passage_ref[...]
        grad_rows_ref[tokens:, :] = grad_query_ref[...]

        @row_loop(rows)
        def _(part):
            grad = grad_rows_ref[part, :]
            embedded, scale = unit_rows(projected_ref[part, :])
            inner = jnp.sum(grad * embedded, axis=-1, keepdims=True)
            grad_low = (scale * (grad - embedded * inner)).astype(jnp.bfloat16)
            grad_low_ref[part, :] = grad_low
            grad_norm = mul_nt(grad_low, project_ref[...])
            unit = unit_two_ref[part, :]
            grad_gain_ref[...] += jnp.sum(grad_norm * unit, axis=0, keepdims=True)
            grad_shift_ref[...] += jnp.sum(grad_norm, axis=0, keepdims=True)
            hidden = norm_backward(grad_norm, unit, scale_two_ref[part, :], gain_ref[...])
            grad_hidden_ref[part, :] = hidden
            branch_ref[part, :] = hidden.astype(jnp.bfloat16)

        grad_project_ref[...] = mul_tn(low_two_ref[...], grad_low_ref[...]).astype(jnp.bfloat16)

    grad_down_ref[...] = mul_tn(active_ref[...], branch_ref[...]).astype(jnp.bfloat16)
    part = rows // ROW_PARTS
    total = None
    for low in range(0, rows, part):
        grad_active = mul_nt(branch_ref[low : low + part, :], down_weight_ref[...])
        pulled = (grad_active * slope_ref[low : low + part, :].astype(jnp.float32)).astype(
            jnp.bfloat16
        )
        grad_up_rows_ref[low : low + part, :] = pulled
        partial = jnp.sum(pulled.astype(jnp.float32), axis=0, keepdims=True)
        total = partial if total is None else total + partial
    grad_bias_ref[...] = total


def down_backward(
    grad_passage,
    grad_query,
    projected,
    low_two,
    unit_two,
    scale_two,
    gain,
    project_weight,
    active,
    slope,
    down_weight,
):
    rows = projected.shape[0]
    tokens = grad_passage.shape[0]
    width = active.shape[1]
    full = fixed_block((rows, D))
    vector = fixed_block((1, D))
    chunk = pl.BlockSpec((rows, FF_TILE), lambda i: (0, i))
    weight = pl.BlockSpec((FF_TILE, D), lambda i: (i, 0))
    bias = pl.BlockSpec((1, FF_TILE), lambda i: (0, i))
    outs = [
        (fixed_block((D, PROJ)), (D, PROJ), jnp.bfloat16),
        (full, (rows, D), jnp.float32),
        (vector, (1, D), jnp.float32),
        (vector, (1, D), jnp.float32),
        (weight, (width, D), jnp.bfloat16),
        (chunk, (rows, width), jnp.bfloat16),
        (bias, (1, width), jnp.float32),
    ]
    return pl.pallas_call(
        down_backward_kernel,
        grid=(width // FF_TILE,),
        in_specs=[
            fixed_block((tokens, PROJ)),
            fixed_block((rows - tokens, PROJ)),
            fixed_block((rows, PROJ)),
            full,
            full,
            fixed_block((rows, 1)),
            vector,
            fixed_block((D, PROJ)),
            chunk,
            chunk,
            weight,
        ],
        out_specs=[spec for spec, _, _ in outs],
        out_shape=[jax.ShapeDtypeStruct(shape, kind) for _, shape, kind in outs],
        scratch_shapes=[
            pltpu.VMEM((rows, PROJ), jnp.bfloat16),
            pltpu.VMEM((rows, D), jnp.bfloat16),
            pltpu.VMEM((rows, PROJ), jnp.float32),
        ],
        name="down_backward",
    )(
        grad_passage,
        grad_query,
        projected,
        low_two,
        unit_two,
        scale_two,
        gain[None],
        project_weight,
        active,
        slope,
        down_weight,
    )


def pack_vectors(vectors, devices, shares):
    packed = jnp.zeros((devices, VECTOR_LANES), jnp.float32)
    start = 0
    for vector, share in zip(vectors, shares):
        count = vector.shape[1]
        device = lax.broadcasted_iota(jnp.int32, (devices, count), 0)
        place = lax.broadcasted_iota(jnp.int32, (devices, count), 1)
        spread = jnp.where(place // share == device, jnp.broadcast_to(vector, place.shape), 0.0)
        source = lax.broadcasted_iota(jnp.int32, (VECTOR_LANES, count), 1)
        lane = lax.broadcasted_iota(jnp.int32, (VECTOR_LANES, count), 0)
        choose = (source % share + start == lane).astype(jnp.float32).astype(jnp.bfloat16)
        high, rest = split_low(spread)
        packed = packed + mul_nt(high, choose) + mul_nt(rest, choose)
        start += share
    return packed


def up_backward_kernel(
    grad_up_rows_ref,
    low_one_ref,
    up_weight_ref,
    grad_hidden_ref,
    unit_one_ref,
    scale_one_ref,
    gain_ref,
    attended_ref,
    grad_second_gain_ref,
    grad_second_shift_ref,
    grad_bias_ref,
    grad_up_ref,
    grad_one_ref,
    branch_ref,
    grad_output_ref,
    vector_ref,
    sum_ref,
    grad_gain_ref,
    grad_shift_ref,
):
    step = pl.program_id(0)
    rows = low_one_ref.shape[0]
    grad_up_ref[...] = mul_tn(low_one_ref[...], grad_up_rows_ref[...]).astype(jnp.bfloat16)
    part = mul_nt(grad_up_rows_ref[...], up_weight_ref[...])

    @pl.when(step == 0)
    def _():
        sum_ref[...] = grad_hidden_ref[...] + part

    @pl.when(step > 0)
    def _():
        sum_ref[...] += part

    @pl.when(step == pl.num_programs(0) - 1)
    def _():
        grad_gain_ref[...] = jnp.zeros_like(grad_gain_ref)
        grad_shift_ref[...] = jnp.zeros_like(grad_shift_ref)

        @row_loop(rows)
        def _(part):
            grad_norm = sum_ref[part, :]
            unit = unit_one_ref[part, :]
            grad_gain_ref[...] += jnp.sum(grad_norm * unit, axis=0, keepdims=True)
            grad_shift_ref[...] += jnp.sum(grad_norm, axis=0, keepdims=True)
            hidden = norm_backward(grad_norm, unit, scale_one_ref[part, :], gain_ref[...])
            grad_one_ref[part, :] = hidden
            branch_ref[part, :] = hidden.astype(jnp.bfloat16)

        grad_output_ref[...] = mul_tn(attended_ref[...], branch_ref[...]).astype(jnp.bfloat16)
        devices, share, _ = vector_ref.shape
        vectors = (
            grad_gain_ref[...],
            grad_shift_ref[...],
            grad_second_gain_ref[...],
            grad_second_shift_ref[...],
            grad_bias_ref[...],
        )
        bias_share = grad_bias_ref.shape[1] // devices
        packed = pack_vectors(vectors, devices, (share,) * 4 + (bias_share,))
        high, rest = split_low(packed)
        row = lax.broadcasted_iota(jnp.int32, vector_ref.shape, 1)
        vector_ref[...] = jnp.where(
            row == 0,
            high.astype(jnp.float32)[:, None, :],
            jnp.where(row == 1, rest.astype(jnp.float32)[:, None, :], 0.0),
        ).astype(jnp.bfloat16)


def up_backward(
    grad_up_rows,
    low_one,
    up_weight,
    grad_hidden,
    unit_one,
    scale_one,
    gain,
    attended,
    grad_second_gain,
    grad_second_shift,
    grad_bias,
    devices,
):
    rows = low_one.shape[0]
    width = up_weight.shape[1]
    full = fixed_block((rows, D))
    vector = fixed_block((1, D))
    weight = pl.BlockSpec((D, FF_TILE), lambda i: (0, i))
    packed = (devices, D // devices, VECTOR_LANES)
    outs = [
        (weight, (D, width), jnp.bfloat16),
        (full, (rows, D), jnp.float32),
        (full, (rows, D), jnp.bfloat16),
        (fixed_block((D, D)), (D, D), jnp.bfloat16),
        (fixed_block(packed), packed, jnp.bfloat16),
    ]
    return pl.pallas_call(
        up_backward_kernel,
        grid=(width // FF_TILE,),
        in_specs=[
            pl.BlockSpec((rows, FF_TILE), lambda i: (0, i)),
            full,
            weight,
            full,
            full,
            fixed_block((rows, 1)),
            vector,
            full,
            vector,
            vector,
            fixed_block((1, width)),
        ],
        out_specs=[spec for spec, _, _ in outs],
        out_shape=[jax.ShapeDtypeStruct(shape, kind) for _, shape, kind in outs],
        scratch_shapes=[
            pltpu.VMEM((rows, D), jnp.float32),
            pltpu.VMEM((1, D), jnp.float32),
            pltpu.VMEM((1, D), jnp.float32),
        ],
        name="up_backward",
    )(
        grad_up_rows,
        low_one,
        up_weight,
        grad_hidden,
        unit_one,
        scale_one,
        gain[None],
        attended,
        grad_second_gain,
        grad_second_shift,
        grad_bias,
    )


def body(
    query_states,
    passage_states,
    passage_bins,
    padding_mask,
    token_ids,
    positives,
    united_weight,
    output_weight,
    first_gain,
    first_shift,
    up_weight,
    up_bias,
    down_weight,
    second_gain,
    second_shift,
    project_weight,
):
    query_count = query_states.shape[0]
    token_count = passage_states.shape[0]
    all_rows = jnp.concatenate([passage_states, query_states], axis=0)
    united_rows = jnp.dot(all_rows, united_weight, preferred_element_type=jnp.float32).astype(
        jnp.bfloat16
    )
    bins_row = passage_bins[0]
    mask_row = padding_mask[0]
    masks = (bins_row[:, None], passage_bins, mask_row[:, None])
    attended, logs = attend_forward(united_rows, masks)
    (
        unit_one,
        scale_one,
        low_one,
        active,
        slope,
        unit_two,
        scale_two,
        low_two,
        projected,
        passage_emb,
        query_emb,
    ) = encode(
        all_rows,
        attended,
        token_count,
        output_weight,
        first_gain,
        first_shift,
        up_weight,
        up_bias,
        down_weight,
        second_gain,
        second_shift,
        project_weight,
    )
    usable = (mask_row == 1) & (token_ids[0] >= SKIP_IDS)
    own_codes = jnp.where(usable, bins_row, -1)
    own_index = lax.axis_index("pb") * lax.axis_size("pa") + lax.axis_index("pa")
    own = own_index.reshape(1)
    queries_here = query_count // QLEN
    blocks = own_index ^ jnp.array(relative_masks(), jnp.int32)
    order = (
        blocks[:, None] * queries_here + lax.broadcasted_iota(jnp.int32, (1, queries_here), 1)
    ).reshape(-1, 1)
    near, far = gather_relative(query_emb)
    code_row = own_codes[None, :]
    wanted = positives[None, :]
    inverse, own_logits = tile_forward(own, near, far, passage_emb, code_row, order, wanted)
    near_logits, far_logits = gather_relative(own_logits)
    grad_near, grad_far, grad_passage_emb, losses = tile_backward(
        own,
        near,
        far,
        passage_emb,
        code_row,
        order,
        wanted,
        inverse,
        own_logits,
        near_logits,
        far_logits,
    )
    own_losses = lax.dynamic_slice_in_dim(losses[0], own_index * queries_here, queries_here)
    grad_query_emb = sum_relative(grad_near, grad_far)
    (
        grad_project,
        grad_hidden_two,
        grad_second_gain,
        grad_second_shift,
        grad_down,
        grad_up_rows,
        grad_up_bias,
    ) = down_backward(
        grad_passage_emb,
        grad_query_emb,
        projected,
        low_two,
        unit_two,
        scale_two,
        second_gain,
        project_weight,
        active,
        slope,
        down_weight,
    )
    down_sum = ScatterSum([grad_down])
    grad_up_rows = start(grad_up_rows, [down_sum])
    devices = lax.axis_size("pb") * lax.axis_size("pa")
    grad_up, grad_hidden_one, grad_branch_one, grad_output, vectors = up_backward(
        grad_up_rows,
        low_one,
        up_weight,
        grad_hidden_two,
        unit_one,
        scale_one,
        first_gain,
        attended,
        grad_second_gain,
        grad_second_shift,
        grad_up_bias,
        devices,
    )
    up_sum = ScatterSum([grad_up, grad_output, grad_project, vectors.reshape(D, -1)], True)
    grad_branch_one = start(grad_branch_one, [up_sum])
    grad_branch_one = meet(grad_branch_one, [down_sum])
    grad_attended = times_transposed(grad_branch_one, output_weight).astype(jnp.bfloat16)
    grad_attended = meet(grad_attended, [up_sum])
    grad_united_rows = attend_backward(united_rows, grad_attended, masks, logs, 0, PAIRS)
    united_sum = ScatterSum([contract_rows(all_rows, grad_united_rows)])
    grad_united_rows = start(grad_united_rows, [united_sum])
    grad_united_rows = meet(grad_united_rows, [down_sum, up_sum])
    grad_rows = times_transposed(grad_united_rows, united_weight) + grad_hidden_one
    united_total = united_sum.finish()
    down_total = down_sum.finish()
    up_total = up_sum.finish()
    width = up_weight.shape[1]
    ends = [width, width + D, width + D + PROJ]
    small = up_total[0] + up_total[1]
    small = small[ends[2] :]
    share = D // devices
    bias_share = width // devices
    shared = (
        united_total,
        up_total[:, ends[0] : ends[1]],
        small[:share],
        small[share : 2 * share],
        up_total[:, :width],
        small[4 * share : 4 * share + bias_share],
        down_total,
        small[2 * share : 3 * share],
        small[3 * share : 4 * share],
        up_total[:, ends[1] : ends[2]],
    )
    return (
        query_emb,
        passage_emb,
        own_losses,
        grad_rows[token_count:],
        grad_rows[:token_count],
        shared[0],
        shared[1],
        shared[2],
        shared[3],
        shared[4],
        shared[5],
        shared[6],
        shared[7],
        shared[8],
        shared[9],
    )


def solution(mesh):
    return jax.shard_map(
        body,
        mesh=mesh,
        in_specs=(
            P(("pb", "pa"), None),
            P(("pb", "pa"), None),
            P(("pb", "pa"), None),
            P(("pb", "pa"), None),
            P(("pb", "pa"), None),
            P(),
            P(),
            P(),
            P(),
            P(),
            P(),
            P(),
            P(),
            P(),
            P(),
            P(),
        ),
        out_specs=(
            P(("pb", "pa"), None),
            P(("pb", "pa"), None),
            P(("pb", "pa")),
            P(("pb", "pa"), None),
            P(("pb", "pa"), None),
            P(("pb", "pa"), None),
            P(("pb", "pa"), None),
            P(("pb", "pa")),
            P(("pb", "pa")),
            P(("pb", "pa"), None),
            P(("pb", "pa")),
            P(("pb", "pa"), None),
            P(("pb", "pa")),
            P(("pb", "pa")),
            P(("pb", "pa"), None),
        ),
        check_vma=False,
    )
```
